32 devices in a mesh: group: 2 (over y), seq: 4 (over z), tensor: 4 (over x, core).
Axes of the slice: x: 2, y: 2, z: 4, core: 2. Of those that a mesh axis runs over, the one named last changes fastest.
Arguments:
- spans: bfloat16 [1024, 3072], P(('group', 'seq')), parts along dimension 0, may hold values from -6 to 6
- w_in: bfloat16 [3072, 1024], P(None, 'tensor'), may hold values from -0.109375 to 0.109375
- band_weights: bfloat16 [4096, 128], P(('group', 'seq')), parts along dimension 0
- offsets: int32 [32], P(('group', 'seq')), parts along dimension 0, may hold values from 0 to 384, as said below
- w_up: bfloat16 [1024, 4096], P(None, 'tensor'), may hold values from -0.1875 to 0.1875
- d_up: bfloat16 [4096, 4096], P(('group', 'seq'), 'tensor'), parts along dimension 0, may hold values from -3 to 3
Outputs:
- up_proj: bfloat16 [4096, 4096], P(('group', 'seq'), 'tensor'), parts along dimension 0
- d_spans: bfloat16 [1024, 3072], P(('group', 'seq'), 'tensor'), parts along dimension 0
The draws below stay inside these ranges and needn't reach their ends.
There are 2 independent parts, one for each index of `group`. The reference program is written for one: setup_inputs(seed, part) draws one part's arguments, and reference() takes and returns one part's arrays. A program takes and returns all parts, laid end to end along the dimension named above; an argument that names none is the same for every part. Nothing has to cross between parts.
Inputs may be any that keep to these rules, and one draw needn't show every extreme that they name: offsets[b] differs from b * 384 // 15 by at most 128, and both differences -128 and +128 occur in every draw; offsets[0] = 0 and offsets[15] = 384. Hence the bands of the bytes of seq index i lie within the span rows of seq indices i - 3 to i + 3.
All inputs are finite; a program needn't handle non-finite values.
Results may differ from the reference program's by a relative error of at most 0.0058.
Values may be sent and summed in bfloat16 or wider, within the bound.
No kernel may reach another device: no remote copies, remote signals or barrier semaphores. Data moves between devices by JAX's collectives and lax.ppermute only.
A program may use at most 64 MiB of HBM per device.

```python
import jax
import jax.numpy as jnp
from jax import lax

DC = 3072
D = 1024
FF = 4096
BLOCK = 128
SPAN_DEV = 128
BYTES = 2048
SPANS = 512


def draw_band_weights(key, part):
    key_rate, key_rough = jax.random.split(key)
    rate_row = jnp.exp(jax.random.uniform(key_rate, (BYTES, 1), jnp.float32, jnp.log(0.01), jnp.log(0.6)))
    roughness = jax.random.uniform(key_rough, (BYTES, BLOCK), jnp.float32, 0.5, 1.5)
    position = (jnp.arange(BYTES, dtype=jnp.int32) % BLOCK)[:, None]
    column_id = jnp.arange(BLOCK, dtype=jnp.int32)[None, :]
    distance = jnp.maximum(position - column_id, 0).astype(jnp.float32)
    inside = position >= column_id
    weights = roughness * rate_row * jnp.exp(jnp.log1p(-rate_row) * distance)
    return jnp.where(inside, weights, 0.0).astype(jnp.bfloat16)


def draw_offsets(key, part):
    blocks = BYTES // BLOCK
    usable = SPANS - BLOCK
    block_id = jnp.arange(blocks, dtype=jnp.int32)
    centre = block_id * usable // (blocks - 1)
    deviation = jax.random.randint(key, (blocks,), -SPAN_DEV, SPAN_DEV + 1, dtype=jnp.int32)
    middle = blocks // 2
    deviation = jnp.where(block_id == middle - 1, -SPAN_DEV, deviation)
    deviation = jnp.where(block_id == middle, SPAN_DEV, deviation)
    placed = jnp.clip(centre + deviation, 0, usable)
    placed = jnp.where(block_id == 0, 0, placed)
    placed = jnp.where(block_id == blocks - 1, usable, placed)
    return placed.astype(jnp.int32)


def level_of(stream_key, shape, shards, low, largest):
    def one(axis_at, parts):
        heights = jax.random.uniform(jax.random.fold_in(jax.random.fold_in(stream_key, 6), axis_at), (parts,), jnp.float32, low / len(shards), largest / len(shards))
        return jnp.repeat(jnp.exp(heights), shape[axis_at] // parts).reshape((-1,) + (1,) * (len(shape) - axis_at - 1))

    gain = one(*shards[0])
    for cut in shards[1:]:
        gain = gain * one(*cut)
    return gain


def centred(rng, dims, scale, most, cuts=(), kind=jnp.bfloat16):
    drawn = jax.random.normal(rng, dims, jnp.float32) * scale
    if len(cuts) > 0:
        drawn = level_of(rng, dims, cuts, -0.22, 0.18) * drawn
    return jnp.clip(drawn, min=-most, max=most).astype(kind)


def setup_inputs(seed: int = 0, part: int = 0) -> dict:
    arg_keys = jax.random.split(jax.random.key(seed), 7)
    part_splits = jax.random.split(jax.random.fold_in(arg_keys[6], part), 7)
    return {
        "spans": centred(part_splits[0], (SPANS, DC), 1.0, 6.0, ((0, 4),)),
        "w_in": centred(arg_keys[1], (DC, D), DC ** -0.5, 0.109375, ((1, 4),)),
        "band_weights": draw_band_weights(jax.random.fold_in(jax.random.fold_in(arg_keys[6], part), 71), part),
        "offsets": draw_offsets(jax.random.fold_in(jax.random.fold_in(arg_keys[6], part), 71), part),
        "w_up": centred(arg_keys[4], (D, FF), D ** -0.5, 0.1875, ((1, 4),)),
        "d_up": centred(part_splits[5], (BYTES, FF), 0.5, 3.0, ((0, 4), (1, 4))),
    }


def reference(spans, w_in, band_weights, offsets, w_up, d_up):
    reduced = jnp.dot(spans, w_in, preferred_element_type=jnp.float32).astype(jnp.bfloat16)
    band_cube = band_weights.reshape(-1, BLOCK, BLOCK)
    starts = offsets.astype(jnp.int32)

    def one_block(block_pair):
        weights, anchor = block_pair
        window = lax.dynamic_slice_in_dim(reduced, anchor.astype(jnp.int32), BLOCK, 0)
        return jnp.dot(weights, window, preferred_element_type=jnp.float32)

    upsampled = lax.map(one_block, (band_cube, starts)).reshape(BYTES, D).astype(jnp.bfloat16)
    up_proj = jnp.dot(upsampled, w_up, preferred_element_type=jnp.float32).astype(jnp.bfloat16)
    grad_upsampled = jnp.dot(d_up, w_up.T, preferred_element_type=jnp.float32).astype(jnp.bfloat16)
    grad_cube = grad_upsampled.reshape(-1, BLOCK, D)

    def scatter_block(running, triple):
        weights, anchor, block_grads = triple
        block_term = jnp.dot(weights.T, block_grads, preferred_element_type=jnp.float32)
        current = lax.dynamic_slice_in_dim(running, anchor.astype(jnp.int32), BLOCK, 0)
        return lax.dynamic_update_slice_in_dim(running, current + block_term, anchor.astype(jnp.int32), 0), None

    d_reduced, unused = lax.scan(scatter_block, jnp.zeros((SPANS, D), jnp.float32), (band_cube, starts, grad_cube))
    d_reduced = d_reduced.astype(jnp.bfloat16)
    d_spans = jnp.dot(d_reduced, w_in.T, preferred_element_type=jnp.float32).astype(jnp.bfloat16)
    return (up_proj, d_spans)
```

```python
import jax
import jax.numpy as jnp
from jax import lax
from jax.sharding import PartitionSpec as P


def reach(seq_count, blocks, breadth, span_rows):
    usable = seq_count * span_rows - breadth
    last = seq_count * blocks - 1
    slack = span_rows
    most = 0
    for index in range(seq_count):
        low = max((index * blocks) * usable // last - slack, 0)
        high = min(((index + 1) * blocks - 1) * usable // last + slack, usable) + breadth
        most = max(most, (index - 1) * span_rows - low, high - (index + 2) * span_rows)
    most = max(16, -(-most // 16) * 16)
    assert most <= span_rows
    return most


def shift(value, count, step):
    pairs = [(i, i + step) for i in range(count) if 0 <= i + step < count]
    return lax.ppermute(value, "seq", pairs)


def swap(value, mask):
    return lax.ppermute(value, "tensor", [(i, i ^ mask) for i in range(4)])


def body(spans, w_in, band_weights, offsets, w_up, d_up):
    f32, bf16 = jnp.float32, jnp.bfloat16
    count = lax.axis_size("seq")
    here = lax.axis_index("tensor")
    blocks, breadth = offsets.shape[0], band_weights.shape[1]
    span_rows = spans.shape[0]
    slice_width = w_in.shape[1]
    far = reach(count, blocks, breadth, span_rows)
    length = 3 * span_rows + 2 * far
    anchor = lax.axis_index("seq") * span_rows - span_rows - far
    first = far + span_rows

    def rows_of(matrix, pieces):
        cube = matrix.reshape(4, -1, matrix.shape[1])
        return jnp.concatenate(
            [lax.dynamic_index_in_dim(cube, here ^ k, 0, keepdims=False) for k in pieces], 0
        )

    reduced = jnp.dot(spans, w_in, preferred_element_type=f32).astype(bf16)
    above = shift(reduced, count, 1)
    below = shift(reduced, count, -1)
    far_above = shift(reduced[span_rows - far :], count, 2)
    far_below = shift(reduced[:far], count, -2)

    w_send = rows_of(w_up, (1, 3))
    w_keep = rows_of(w_up, (0, 2))
    over_hidden = (((1,), (1,)), ((), ()))
    grad_sent = lax.dot_general(d_up, w_send, over_hidden, preferred_element_type=f32).astype(bf16)
    grad_got = swap(grad_sent, 1)

    relative = anchor + jnp.arange(length, dtype=jnp.int32)[None, :] - offsets[:, None]
    picker = (relative[:, None, :] == jnp.arange(breadth, dtype=jnp.int32)[None, :, None]).astype(bf16)
    band_cube = band_weights.reshape(blocks, -1, breadth)
    spread = (
        jnp.einsum("bij,bjr->bir", band_cube, picker, preferred_element_type=f32)
        .astype(bf16)
        .reshape(-1, length)
    )

    window = jnp.concatenate([far_above, above, reduced, below, far_below], 0)
    upsampled = jnp.dot(spread, window, preferred_element_type=f32).astype(bf16)
    up_x = swap(upsampled, 2)
    up_core = swap(upsampled, 1)

    grad_kept = lax.dot_general(d_up, w_keep, over_hidden, preferred_element_type=f32)
    grad = (grad_kept + grad_got.astype(f32)).astype(bf16)
    shares = lax.dot_general(spread, grad, (((0,), (0,)), ((), ())), preferred_element_type=f32)
    sent = shares.astype(bf16)
    from_below = shift(sent[far:first], count, -1)
    from_above = shift(sent[first + span_rows : first + 2 * span_rows], count, 1)
    from_far_below = shift(sent[:far], count, -2)
    from_far_above = shift(sent[first + 2 * span_rows :], count, 2)
    total = shares[first : first + span_rows] + from_below.astype(f32) + from_above.astype(f32)
    rest = span_rows - far
    total = total + jnp.pad(from_far_below.astype(f32), ((rest, 0), (0, 0)))
    total = total + jnp.pad(from_far_above.astype(f32), ((0, rest), (0, 0)))

    over_x = swap(total[:, slice_width:].astype(bf16), 2)
    d_reduced = (total[:, :slice_width] + over_x.astype(f32)).astype(bf16)

    def parts(k):
        return lax.dot_general(
            d_reduced, rows_of(w_in, (k,)), over_hidden, preferred_element_type=f32
        )

    part_x = parts(2) + swap(parts(3).astype(bf16), 1).astype(f32)
    other_x = swap(part_x.astype(bf16), 2)
    part = parts(0) + swap(parts(1).astype(bf16), 1).astype(f32)
    d_spans = (part + other_x.astype(f32)).astype(bf16)

    up_x_core = swap(up_x, 1)
    gathered = jnp.concatenate([upsampled, up_core, up_x, up_x_core], 1)
    up_proj = jnp.dot(
        gathered, rows_of(w_up, (0, 1, 2, 3)), preferred_element_type=f32
    ).astype(bf16)
    return (up_proj, d_spans)


def solution(mesh):
    placed = (
        P(("group", "seq"), None),
        P(None, "tensor"),
        P(("group", "seq"), None),
        P(("group", "seq")),
        P(None, "tensor"),
        P(("group", "seq"), "tensor"),
    )
    return jax.shard_map(
        body,
        mesh=mesh,
        in_specs=placed,
        out_specs=(P(("group", "seq"), "tensor"), P(("group", "seq"), "tensor")),
        check_vma=False,
    )
```

```python
import jax
import jax.numpy as jnp
from jax import lax
from jax.experimental import pallas as pl
from jax.experimental.pallas import tpu as pltpu
from jax.sharding import PartitionSpec as P

F32, BF16 = jnp.float32, jnp.bfloat16
NOWHERE = -(1 << 20)


def reach(count, blocks, breadth, span_rows):
    usable = count * span_rows - breadth
    last = count * blocks - 1
    most = 0
    for index in range(count):
        low = max(index * blocks * usable // last - span_rows, 0)
        high = min(((index + 1) * blocks - 1) * usable // last + span_rows, usable) + breadth
        most = max(most, (index - 1) * span_rows - low, high - (index + 2) * span_rows)
    most = max(16, -(-most // 16) * 16)
    assert most <= span_rows
    return most


def pairings(count):
    found = []
    for distance in (1, 2):
        for parity in (0, 1):
            if any(partner(i, distance, parity, count) != i for i in range(count)):
                found.append((distance, parity))
    return found


def partner(index, distance, parity, count):
    up = (index // distance) % 2 == parity
    other = index + distance if up else index - distance
    return other if 0 <= other < count else index


def partner_here(distance, parity, count):
    index = lax.axis_index("seq")
    up = lax.rem(lax.div(index, distance), 2) == parity
    other = jnp.where(up, index + distance, index - distance)
    return other, up, (other >= 0) & (other < count)


def trade(value, pairing, count):
    return lax.ppermute(value, "seq", [(i, partner(i, *pairing, count)) for i in range(count)])


def swap(value, mask):
    return lax.ppermute(value, "tensor", [(i, i ^ mask) for i in range(4)])


def call(kernel, outs, *args, flops, scalars=()):
    moved = sum(a.size * a.dtype.itemsize for a in args)
    moved += sum(o.size * o.dtype.itemsize for o in outs)
    spaces = [pltpu.SMEM if k in scalars else pltpu.VMEM for k in range(len(args))]
    got = pl.pallas_call(
        kernel,
        out_shape=outs,
        in_specs=[pl.BlockSpec(memory_space=s) for s in spaces],
        out_specs=[pl.BlockSpec(memory_space=pltpu.VMEM) for _ in outs],
        compiler_params=pltpu.CompilerParams(vmem_limit_bytes=16 << 20),
        cost_estimate=pl.CostEstimate(flops=flops, bytes_accessed=moved, transcendentals=0),
    )(*args)
    return got


def shape(dims, kind=BF16):
    return jax.ShapeDtypeStruct(dims, kind)


def dot(a, b):
    return jnp.dot(a, b, preferred_element_type=F32)


def dot_t(a, b):
    return lax.dot_general(a, b, (((1,), (1,)), ((), ())), preferred_element_type=F32)


def body(spans, w_in, band_weights, offsets, w_up, d_up):
    count = lax.axis_size("seq")
    groups = lax.axis_size("group")
    blocks, breadth = offsets.shape[0], band_weights.shape[1]
    bytes_here, hidden = d_up.shape
    block = bytes_here // blocks
    span_rows, depth = spans.shape
    width = w_in.shape[1]
    share = depth // 4
    far = reach(count, blocks, breadth, span_rows)
    pairs = pairings(count)
    rows = [span_rows] + [span_rows if d == 1 else far for d, _ in pairs]
    cols = [breadth * k for k in range(len(rows))]
    longs = [p for p in pairs if p[0] == 2]

    def cut_at(distance, parity):
        _, up, _ = partner_here(distance, parity, count)
        return pl.multiple_of(jnp.where(up, span_rows - far, 0), 16)

    def block_of(ref, mask, size):
        at = (lax.axis_index("tensor") ^ mask) * size
        return ref[pl.ds(pl.multiple_of(at, size), size), :]

    here = lax.axis_index("tensor")
    cube = w_in.reshape(4, share, width)

    def quarter(index):
        return lax.dynamic_index_in_dim(cube, index, 0, keepdims=False)

    half = lax.axis_index("group") if groups == 2 else 0
    w_core = swap(quarter(here ^ 1), 1)
    if groups == 2:
        w_x = swap(quarter((here ^ 2) ^ half), 2)
        ring = []
        for t in range(4):
            ring += [(t, 4 + t), (4 + t, t ^ 1)]
        w_ring = lax.ppermute(w_x, ("group", "tensor"), ring)
        w_side = swap(w_x, 1)
    else:
        w_x = swap(quarter(here ^ 2), 2)
        w_ring = swap(quarter(here ^ 3), 3)
        w_side = w_ring

    def project(spans_ref, w_ref, out_ref, *cut_refs):
        out_ref[...] = dot(spans_ref[...], w_ref[...]).astype(BF16)
        for ref, pairing in zip(cut_refs, longs):
            ref[...] = out_ref[pl.ds(cut_at(*pairing), far), :]

    reduced, *cuts = call(
        project,
        [shape((span_rows, width))] + [shape((far, width)) for _ in longs],
        spans,
        w_in,
        flops=2 * span_rows * depth * width,
    )
    sends = [reduced for _ in pairs if _[0] == 1] + cuts
    pieces = [reduced] + [trade(s, p, count) for s, p in zip(sends, pairs)]

    def grad_part(masks, kind):
        def kernel(d_ref, w_ref, out_ref):
            for k, mask in enumerate(masks):
                part = dot_t(d_ref[...], block_of(w_ref, mask, width))
                out_ref[:, k * width : (k + 1) * width] = part.astype(kind)

        return call(
            kernel,
            [shape((bytes_here, 2 * width), kind)],
            d_up,
            w_up,
            flops=4 * bytes_here * width * hidden,
        )[0]

    grad_got = swap(grad_part((1, 3), BF16), 1)
    grad_kept = grad_part((0, 2), F32)

    def spread(off_ref, weights_ref, band_ref, turned_ref):
        starts = [lax.axis_index("seq") * span_rows]
        for distance, parity in pairs:
            other, up, there = partner_here(distance, parity, count)
            skip = 0 if distance == 1 else jnp.where(up, 0, span_rows - far)
            starts.append(jnp.where(there, other * span_rows + skip, NOWHERE))
        down = lax.broadcasted_iota(jnp.int32, (breadth, breadth), 0)
        across = lax.broadcasted_iota(jnp.int32, (breadth, breadth), 1)
        for b in range(blocks):
            part = slice(b * block, (b + 1) * block)
            weights = weights_ref[part, :]
            for k, (start, size) in enumerate(zip(starts, rows)):
                piece = slice(cols[k], cols[k] + breadth)
                gap = start - off_ref[b]
                pick = ((across + gap == down) & (across < size)).astype(F32).astype(BF16)
                band_ref[part, piece] = dot(weights, pick).astype(BF16)
                pick = ((down + gap == across) & (down < size)).astype(F32).astype(BF16)
                turned_ref[piece, part] = dot_t(pick, weights).astype(BF16)

    total_cols = breadth * len(rows)
    band, turned = call(
        spread,
        [shape((bytes_here, total_cols)), shape((total_cols, bytes_here))],
        offsets,
        band_weights,
        flops=4 * bytes_here * breadth * total_cols,
        scalars=(0,),
    )

    def spread_grad(kept_ref, got_ref, turned_ref, own_ref, *out_refs):
        grad = (kept_ref[...] + got_ref[...].astype(F32)).astype(BF16)
        for k, ref in enumerate((own_ref,) + out_refs):
            part = dot(turned_ref[cols[k] : cols[k] + rows[k], :], grad)
            ref[...] = part.astype(ref.dtype)

    own, *shares = call(
        spread_grad,
        [shape((r, 2 * width), F32 if k == 0 else BF16) for k, r in enumerate(rows)],
        grad_kept,
        grad_got,
        turned,
        flops=4 * bytes_here * width * sum(rows),
    )
    came = [trade(s, p, count) for s, p in zip(shares, pairs)]

    def upsample(band_ref, *refs):
        *piece_refs, out_ref = refs
        acc = 0.0
        for k, ref in enumerate(piece_refs):
            acc += dot(band_ref[:, cols[k] : cols[k] + rows[k]], ref[...])
        out_ref[...] = acc.astype(BF16)

    (upsampled,) = call(
        upsample,
        [shape((bytes_here, width))],
        band,
        *pieces,
        flops=2 * bytes_here * width * sum(rows),
    )
    up_x = swap(upsampled, 2)
    up_core = swap(upsampled, 1)
    up_both = swap(up_x, 1)

    def collect(own_ref, *refs):
        *came_refs, sum_ref, sent_ref = refs
        sum_ref[...] = own_ref[...]
        for ref, (distance, parity) in zip(came_refs, pairs):
            if distance == 1:
                sum_ref[...] += ref[...].astype(F32)
            else:
                sum_ref[pl.ds(cut_at(distance, parity), far), :] += ref[...].astype(F32)
        sent_ref[:, width:] = sum_ref[:, :width].astype(BF16)
        sent_ref[:, :width] = sum_ref[:, width:].astype(BF16)

    summed, sent = call(
        collect,
        [shape((span_rows, 2 * width), F32), shape((span_rows, 2 * width))],
        own,
        *came,
        flops=8 * span_rows * width,
    )
    d_reduced = (summed + swap(sent, 2).astype(F32)).astype(BF16)
    d_other = swap(d_reduced, 1)

    def finish(mine_ref, other_ref, w_ref, core_ref, x_ref, ring_ref, side_ref, out_ref):
        acc = dot_t(mine_ref[:, :width], block_of(w_ref, 0, share))
        acc += dot_t(other_ref[:, :width], core_ref[...])
        if groups == 2:
            first = lax.axis_index("group") == 0
            near = jnp.where(first, x_ref[...], ring_ref[...])
            cross = jnp.where(first, ring_ref[...], side_ref[...])
        else:
            near, cross = x_ref[...], ring_ref[...]
        acc += dot_t(mine_ref[:, width:], near)
        acc += dot_t(other_ref[:, width:], cross)
        out_ref[...] = acc.astype(BF16)

    (d_spans,) = call(
        finish,
        [shape((span_rows, share))],
        d_reduced,
        d_other,
        w_in,
        w_core,
        w_x,
        w_ring,
        w_side,
        flops=8 * span_rows * width * share,
    )

    def up_project(a_ref, b_ref, c_ref, d_ref, w_ref, out_ref):
        acc = 0.0
        for mask, ref in enumerate((a_ref, b_ref, c_ref, d_ref)):
            acc += dot(ref[...], block_of(w_ref, mask, width))
        out_ref[...] = acc.astype(BF16)

    (up_proj,) = call(
        up_project,
        [shape((bytes_here, hidden))],
        upsampled,
        up_core,
        up_x,
        up_both,
        w_up,
        flops=8 * bytes_here * width * hidden,
    )
    return (up_proj, d_spans)


def solution(mesh):
    placed = (
        P(("group", "seq"), None),
        P(None, "tensor"),
        P(("group", "seq"), None),
        P(("group", "seq")),
        P(None, "tensor"),
        P(("group", "seq"), "tensor"),
    )
    return jax.shard_map(
        body,
        mesh=mesh,
        in_specs=placed,
        out_specs=(P(("group", "seq"), "tensor"), P(("group", "seq"), "tensor")),
        check_vma=False,
    )
```

```python
import functools

import jax
import jax.numpy as jnp
from jax import lax
from jax.experimental import pallas as pl
from jax.experimental.pallas import tpu as pltpu
from jax.sharding import PartitionSpec as P

F32, BF16 = jnp.float32, jnp.bfloat16
NOWHERE = -(1 << 20)


def reach(count, blocks, breadth, span_rows):
    usable = count * span_rows - breadth
    last = count * blocks - 1
    most = 0
    for index in range(count):
        low = max(index * blocks * usable // last - span_rows, 0)
        high = min(((index + 1) * blocks - 1) * usable // last + span_rows, usable) + breadth
        most = max(most, (index - 1) * span_rows - low, high - (index + 2) * span_rows)
    most = max(16, -(-most // 16) * 16)
    assert most <= span_rows
    return most


def pairings(count):
    every = [(1, 1), (2, 0), (2, 1), (1, 0)]
    return [p for p in every if any(partner(i, *p, count) != i for i in range(count))]


def partner(index, distance, parity, count):
    up = (index // distance) % 2 == parity
    other = index + distance if up else index - distance
    return other if 0 <= other < count else index


def partner_here(distance, parity, count):
    index = lax.axis_index("seq")
    up = lax.rem(lax.div(index, distance), 2) == parity
    other = jnp.where(up, index + distance, index - distance)
    return other, up, (other >= 0) & (other < count)


def trade(value, pairing, count):
    pairs = []
    for i in range(count):
        other = partner(i, *pairing, count)
        for t in range(4):
            pairs.append((4 * i + t, 4 * other + (t ^ 1 if other == i else t)))
    return lax.ppermute(value, ("seq", "tensor"), pairs)


def swap(value, mask):
    return lax.ppermute(value, "tensor", [(i, i ^ mask) for i in range(4)])


def call(kernel, outs, *args, flops, scalars=(), after=()):
    moved = sum(a.size * a.dtype.itemsize for a in args)
    moved += sum(o.size * o.dtype.itemsize for o in outs)
    spaces = [pltpu.SMEM if k in scalars else pltpu.VMEM for k in range(len(args))]
    spaces += [pl.ANY] * len(after)
    inputs = len(args)

    def run(*refs):
        kernel(*refs[:inputs], *refs[inputs + len(after) : -1])
        refs[-1][...] = jnp.zeros_like(refs[-1])

    return pl.pallas_call(
        run,
        out_shape=list(outs) + [shape((8, 128), F32)],
        name=getattr(kernel, "func", kernel).__name__,
        in_specs=[pl.BlockSpec(memory_space=space) for space in spaces],
        out_specs=[pl.BlockSpec(memory_space=pltpu.VMEM)] * (len(outs) + 1),
        compiler_params=pltpu.CompilerParams(vmem_limit_bytes=16 << 20),
        cost_estimate=pl.CostEstimate(flops=flops, bytes_accessed=moved, transcendentals=0),
    )(*args, *after)


def shape(dims, kind=BF16):
    return jax.ShapeDtypeStruct(dims, kind)


def dot(a, b):
    return jnp.dot(a, b, preferred_element_type=F32)


def dot_t(a, b):
    return lax.dot_general(a, b, (((1,), (1,)), ((), ())), preferred_element_type=F32)


def body(spans, w_in, band_weights, offsets, w_up, d_up):
    count = lax.axis_size("seq")
    groups = lax.axis_size("group")
    blocks, breadth = offsets.shape[0], band_weights.shape[1]
    bytes_here, hidden = d_up.shape
    block = bytes_here // blocks
    span_rows, depth = spans.shape
    width = w_in.shape[1]
    share = depth // 4
    far = reach(count, blocks, breadth, span_rows)
    pairs = pairings(count)
    rows = [span_rows] + [span_rows if d == 1 else far for d, _ in pairs]
    cols = [breadth * k for k in range(len(rows))]
    longs = [p for p in pairs if p[0] == 2]

    def cut_at(distance, parity):
        _, up, _ = partner_here(distance, parity, count)
        return pl.multiple_of(jnp.where(up, span_rows - far, 0), 16)

    def block_of(ref, mask, size):
        at = (lax.axis_index("tensor") ^ mask) * size
        return ref[pl.ds(pl.multiple_of(at, size), size), :]

    here = lax.axis_index("tensor")
    cube = w_in.reshape(4, share, width)

    def quarter(index):
        return lax.dynamic_index_in_dim(cube, index, 0, keepdims=False)

    half = lax.axis_index("group") if groups == 2 else 0
    w_core = swap(quarter(here ^ 1), 1)
    w_x_sent = quarter(here ^ 2 ^ half)
    w_x = swap(w_x_sent, 2)

    total_cols = breadth * len(rows)

    def grad_part(masks, d_ref, w_ref, out_ref):
        for k, mask in enumerate(masks):
            part = dot_t(d_ref[...], block_of(w_ref, mask, width))
            out_ref[:, k * width : (k + 1) * width] = part.astype(out_ref.dtype)

    def spread(off_ref, weights_ref, band_ref, turned_ref):
        starts = [lax.axis_index("seq") * span_rows]
        for distance, parity in pairs:
            other, up, there = partner_here(distance, parity, count)
            skip = 0 if distance == 1 else jnp.where(up, 0, span_rows - far)
            starts.append(jnp.where(there, other * span_rows + skip, NOWHERE))

        def row_ids(along):
            dims = (breadth, total_cols) if along else (total_cols, breadth)
            at = lax.broadcasted_iota(jnp.int32, dims, along)
            ids = NOWHERE
            for start, size, col in zip(starts, rows, cols):
                ids = jnp.where((at >= col) & (at < col + size), at + (start - col), ids)
            return ids, lax.broadcasted_iota(jnp.int32, dims, 1 - along)

        across, down_j = row_ids(1)
        down, across_j = row_ids(0)
        for b in range(blocks):
            part = slice(b * block, (b + 1) * block)
            weights = weights_ref[part, :]
            pick = (across - off_ref[b] == down_j).astype(F32).astype(BF16)
            band_ref[part, :] = dot(weights, pick).astype(BF16)
            pick = (down - off_ref[b] == across_j).astype(F32).astype(BF16)
            turned_ref[:, part] = dot_t(pick, weights).astype(BF16)

    def open_up(
        off_hbm, weights_hbm, d_hbm, w_hbm, band_ref, turned_ref, out_ref, token_ref, off, weights, d_vm, w_vm, sems
    ):
        at = lax.axis_index("tensor")
        loads = []

        def load(source, target):
            copy = pltpu.make_async_copy(source, target, sems.at[len(loads)])
            copy.start()
            loads.append(copy)

        load(off_hbm, off)
        load(weights_hbm, weights)
        for k, mask in enumerate((1, 3)):
            part = pl.ds(pl.multiple_of((at ^ mask) * width, width), width)
            load(w_hbm.at[part, :], w_vm.at[k])
            step = bytes_here // 4
            for q in (2 * k, 2 * k + 1):
                part = pl.ds(q * step, step)
                load(d_hbm.at[part, :], d_vm.at[part, :])
        for copy in loads[:2]:
            copy.wait()
        token_ref[...] = jnp.zeros_like(token_ref)
        spread(off, weights, band_ref, turned_ref)
        for copy in loads[2:]:
            copy.wait()
        for k in range(2):
            out_ref[:, k * width : (k + 1) * width] = dot_t(d_vm[...], w_vm[k]).astype(BF16)

    def fixed(value):
        return pltpu.with_memory_space_constraint(value, pltpu.HBM)

    band, turned, grad_sent, opened = pl.pallas_call(
        open_up,
        out_shape=[
            shape((bytes_here, total_cols)),
            shape((total_cols, bytes_here)),
            shape((bytes_here, 2 * width)),
            shape((8, 128), F32),
        ],
        in_specs=[pl.BlockSpec(memory_space=pltpu.HBM)] * 4,
        out_specs=[pl.BlockSpec(memory_space=pltpu.VMEM)] * 4,
        scratch_shapes=[
            pltpu.SMEM((blocks,), jnp.int32),
            pltpu.VMEM((bytes_here, breadth), BF16),
            pltpu.VMEM((bytes_here, hidden), BF16),
            pltpu.VMEM((2, width, hidden), BF16),
            pltpu.SemaphoreType.DMA((8,)),
        ],
        name="open_up",
        compiler_params=pltpu.CompilerParams(vmem_limit_bytes=16 << 20),
        cost_estimate=pl.CostEstimate(
            flops=4 * bytes_here * width * hidden,
            bytes_accessed=2 * (2 * width + bytes_here) * hidden,
            transcendentals=0,
        ),
    )(fixed(offsets), fixed(band_weights), fixed(d_up), fixed(w_up))
    grad_got = swap(grad_sent, 1)

    def project(spans_ref, w_ref, out_ref, *cut_refs):
        out_ref[...] = dot(spans_ref[...], w_ref[...]).astype(BF16)
        for ref, pairing in zip(cut_refs, longs):
            ref[...] = out_ref[pl.ds(cut_at(*pairing), far), :]

    reduced, *cuts, reduced_done = call(
        project,
        [shape((span_rows, width))] + [shape((far, width)) for _ in longs],
        spans,
        w_in,
        flops=2 * span_rows * depth * width,
        after=(opened,),
    )
    cut_of = dict(zip(longs, cuts))
    pieces = [reduced] + [trade(cut_of.get(p, reduced), p, count) for p in pairs]

    grad_kept, _ = call(
        functools.partial(grad_part, (0, 2)),
        [shape((bytes_here, 2 * width), F32)],
        d_up,
        w_up,
        flops=4 * bytes_here * width * hidden,
        after=(reduced_done,),
    )

    def part_of(turned_ref, k, grad):
        return dot(turned_ref[cols[k] : cols[k] + rows[k], :], grad)

    def first_share(kept_ref, got_ref, turned_ref, grad_ref, out_ref):
        grad_ref[...] = (kept_ref[...] + got_ref[...].astype(F32)).astype(BF16)
        out_ref[...] = part_of(turned_ref, 1, grad_ref[...]).astype(BF16)

    def next_share(k, grad_ref, turned_ref, out_ref):
        out_ref[...] = part_of(turned_ref, k, grad_ref[...]).astype(out_ref.dtype)

    products = [2 * bytes_here * 2 * width * r for r in rows]
    grad, share_sent, share_done = call(
        first_share,
        [shape((bytes_here, 2 * width)), shape((rows[1], 2 * width))],
        grad_kept,
        grad_got,
        turned,
        flops=products[1],
    )
    came = [trade(share_sent, pairs[0], count)]
    for k in range(2, len(rows)):
        share_sent, share_done = call(
            functools.partial(next_share, k),
            [shape((rows[k], 2 * width))],
            grad,
            turned,
            flops=products[k],
            after=(share_done,),
        )
        came.append(trade(share_sent, pairs[k - 1], count))
    own, own_done = call(
        functools.partial(next_share, 0),
        [shape((span_rows, 2 * width), F32)],
        grad,
        turned,
        flops=products[0],
        after=(share_done,),
    )

    if groups == 2:
        ring = []
        for t in range(4):
            ring += [(t, 4 + t), (4 + t, t ^ 1)]
        w_ring = lax.ppermute(w_x, ("group", "tensor"), ring)
        w_side = swap(w_x, 1)
    else:
        w_ring = swap(quarter(here ^ 3), 3)
        w_side = w_ring

    def upsample(band_ref, *refs):
        *piece_refs, out_ref = refs
        acc = 0.0
        for k, ref in enumerate(piece_refs):
            acc += dot(band_ref[:, cols[k] : cols[k] + rows[k]], ref[...])
        out_ref[...] = acc.astype(BF16)

    upsampled, _ = call(
        upsample,
        [shape((bytes_here, width))],
        band,
        *pieces,
        flops=2 * bytes_here * width * sum(rows),
        after=(own_done,),
    )
    up_x = swap(upsampled, 2)
    up_core = swap(upsampled, 1)

    def collect(own_ref, *refs):
        *came_refs, sum_ref, sent_ref = refs
        sum_ref[...] = own_ref[...]
        for ref, (distance, parity) in zip(came_refs, pairs):
            if distance == 1:
                sum_ref[...] += ref[...].astype(F32)
            else:
                sum_ref[pl.ds(cut_at(distance, parity), far), :] += ref[...].astype(F32)
        sent_ref[:, width:] = sum_ref[:, :width].astype(BF16)
        sent_ref[:, :width] = sum_ref[:, width:].astype(BF16)

    summed, sent, _ = call(
        collect,
        [shape((span_rows, 2 * width), F32), shape((span_rows, 2 * width))],
        own,
        *came,
        flops=8 * span_rows * width,
    )
    over_x = swap(sent, 2)
    up_x, summed = lax.optimization_barrier((up_x, summed))
    up_both = swap(up_x, 1)

    def up_project(a_ref, b_ref, c_ref, d_ref, w_ref, ring_ref, out_hbm, out_vm, sems):
        refs = (a_ref, b_ref, c_ref, d_ref)
        step = bytes_here // 4
        copies = []
        for q in range(4):
            part = slice(q * step, (q + 1) * step)
            acc = 0.0
            for mask, ref in enumerate(refs):
                acc += dot(ref[part, :], block_of(w_ref, mask, width))
            out_vm[part, :] = acc.astype(BF16)
            part = pl.ds(q * step, step)
            copies.append(pltpu.make_async_copy(out_vm.at[part, :], out_hbm.at[part, :], sems.at[q]))
            copies[-1].start()
        for copy in copies:
            copy.wait()

    up_proj = pl.pallas_call(
        up_project,
        out_shape=shape((bytes_here, hidden)),
        in_specs=[pl.BlockSpec(memory_space=pltpu.VMEM)] * 5 + [pl.BlockSpec(memory_space=pl.ANY)],
        out_specs=pl.BlockSpec(memory_space=pltpu.HBM),
        scratch_shapes=[pltpu.VMEM((bytes_here, hidden), BF16), pltpu.SemaphoreType.DMA((4,))],
        name="up_project",
        compiler_params=pltpu.CompilerParams(vmem_limit_bytes=16 << 20),
        cost_estimate=pl.CostEstimate(
            flops=8 * bytes_here * width * hidden,
            bytes_accessed=2 * bytes_here * hidden,
            transcendentals=0,
        ),
    )(upsampled, up_core, up_x, up_both, w_up, w_ring)

    summed, up_proj = lax.optimization_barrier((summed, up_proj))
    d_reduced = (summed + over_x.astype(F32)).astype(BF16)
    d_other = swap(d_reduced, 1)

    def finish_mine(mine_ref, w_ref, x_ref, ring_ref, out_ref):
        near = x_ref[...]
        if groups == 2:
            near = jnp.where(lax.axis_index("group") == 0, near, ring_ref[...])
        part = dot_t(mine_ref[:, :width], block_of(w_ref, 0, share))
        out_ref[...] = part + dot_t(mine_ref[:, width:], near)

    def finish(part_ref, other_ref, core_ref, ring_ref, side_ref, out_ref):
        cross = ring_ref[...]
        if groups == 2:
            cross = jnp.where(lax.axis_index("group") == 0, cross, side_ref[...])
        part = part_ref[...] + dot_t(other_ref[:, :width], core_ref[...])
        out_ref[...] = (part + dot_t(other_ref[:, width:], cross)).astype(BF16)

    work = 4 * span_rows * width * share
    mine, _ = call(
        finish_mine, [shape((span_rows, share), F32)], d_reduced, w_in, w_x, w_ring, flops=work
    )
    d_spans, _ = call(
        finish, [shape((span_rows, share))], mine, d_other, w_core, w_ring, w_side, flops=work
    )

    return (up_proj, d_spans)


def solution(mesh):
    placed = (
        P(("group", "seq"), None),
        P(None, "tensor"),
        P(("group", "seq"), None),
        P(("group", "seq")),
        P(None, "tensor"),
        P(("group", "seq"), "tensor"),
    )
    return jax.shard_map(
        body,
        mesh=mesh,
        in_specs=placed,
        out_specs=(P(("group", "seq"), "tensor"), P(("group", "seq"), "tensor")),
        check_vma=False,
    )
```

```python
import functools

import jax
import jax.numpy as jnp
from jax import lax
from jax.experimental import pallas as pl
from jax.experimental.pallas import tpu as pltpu
from jax.sharding import PartitionSpec as P

F32, BF16 = jnp.float32, jnp.bfloat16
NOWHERE = -(1 << 20)


def reach(count, blocks, breadth, span_rows):
    usable = count * span_rows - breadth
    last = count * blocks - 1
    most = 0
    for index in range(count):
        low = max(index * blocks * usable // last - span_rows, 0)
        high = min(((index + 1) * blocks - 1) * usable // last + span_rows, usable) + breadth
        most = max(most, (index - 1) * span_rows - low, high - (index + 2) * span_rows)
    most = max(16, -(-most // 16) * 16)
    assert most <= span_rows
    return most


def pairings(count):
    every = [(1, 1), (2, 0), (2, 1), (1, 0)]
    return [p for p in every if any(partner(i, *p, count) != i for i in range(count))]


def partner(index, distance, parity, count):
    up = (index // distance) % 2 == parity
    other = index + distance if up else index - distance
    return other if 0 <= other < count else index


def partner_here(distance, parity, count):
    index = lax.axis_index("seq")
    up = lax.rem(lax.div(index, distance), 2) == parity
    other = jnp.where(up, index + distance, index - distance)
    return other, up, (other >= 0) & (other < count)


def trade(value, pairing, count):
    pairs = []
    for i in range(count):
        other = partner(i, *pairing, count)
        for t in range(4):
            pairs.append((4 * i + t, 4 * other + (t ^ 1 if other == i else t)))
    return lax.ppermute(value, ("seq", "tensor"), pairs)


def swap(value, mask):
    return lax.ppermute(value, "tensor", [(i, i ^ mask) for i in range(4)])


def call(kernel, outs, *args, flops, after=(), token=False):
    moved = sum(a.size * a.dtype.itemsize for a in args)
    moved += sum(o.size * o.dtype.itemsize for o in outs)
    spaces = [pltpu.VMEM] * len(args) + [pl.ANY] * len(after)
    inputs = len(args)
    outs = list(outs) + [shape((8, 128), F32)] * token

    def run(*refs):
        results = refs[inputs + len(after) :]
        if token:
            *results, token_ref = results
            token_ref[...] = jnp.zeros_like(token_ref)
        kernel(*refs[:inputs], *results)

    return pl.pallas_call(
        run,
        out_shape=outs,
        name=getattr(kernel, "func", kernel).__name__,
        in_specs=[pl.BlockSpec(memory_space=space) for space in spaces],
        out_specs=[pl.BlockSpec(memory_space=pltpu.VMEM)] * len(outs),
        compiler_params=pltpu.CompilerParams(vmem_limit_bytes=16 << 20),
        cost_estimate=pl.CostEstimate(flops=flops, bytes_accessed=moved, transcendentals=0),
    )(*args, *after)


def shape(dims, kind=BF16):
    return jax.ShapeDtypeStruct(dims, kind)


def dot(a, b):
    return jnp.dot(a, b, preferred_element_type=F32)


def dot_t(a, b):
    return lax.dot_general(a, b, (((1,), (1,)), ((), ())), preferred_element_type=F32)


def body(spans, w_in, band_weights, offsets, w_up, d_up):
    count = lax.axis_size("seq")
    groups = lax.axis_size("group")
    blocks, breadth = offsets.shape[0], band_weights.shape[1]
    bytes_here, hidden = d_up.shape
    block = bytes_here // blocks
    span_rows, depth = spans.shape
    width = w_in.shape[1]
    share = depth // 4
    far = reach(count, blocks, breadth, span_rows)
    pairs = pairings(count)
    rows = [span_rows] + [span_rows if d == 1 else far for d, _ in pairs]
    cols = [breadth * k for k in range(len(rows))]
    longs = [p for p in pairs if p[0] == 2]

    def cut_at(distance, parity):
        _, up, _ = partner_here(distance, parity, count)
        return pl.multiple_of(jnp.where(up, span_rows - far, 0), 16)

    def block_of(ref, mask, size):
        at = (lax.axis_index("tensor") ^ mask) * size
        return ref[pl.ds(pl.multiple_of(at, size), size), :]

    total_cols = breadth * len(rows)

    def grad_part(masks, d_ref, w_ref, out_ref):
        for k, mask in enumerate(masks):
            part = dot_t(d_ref[...], block_of(w_ref, mask, width))
            out_ref[:, k * width : (k + 1) * width] = part.astype(out_ref.dtype)

    def spread(off_ref, weights_ref, band_ref, turned_ref):
        starts = [lax.axis_index("seq") * span_rows]
        for distance, parity in pairs:
            other, up, there = partner_here(distance, parity, count)
            skip = 0 if distance == 1 else jnp.where(up, 0, span_rows - far)
            starts.append(jnp.where(there, other * span_rows + skip, NOWHERE))

        def row_ids(along):
            dims = (breadth, total_cols) if along else (total_cols, breadth)
            at = lax.broadcasted_iota(jnp.int32, dims, along)
            ids = NOWHERE
            for start, size, col in zip(starts, rows, cols):
                ids = jnp.where((at >= col) & (at < col + size), at + (start - col), ids)
            return ids, lax.broadcasted_iota(jnp.int32, dims, 1 - along)

        across, down_j = row_ids(1)
        down, across_j = row_ids(0)
        for b in range(blocks):
            part = slice(b * block, (b + 1) * block)
            weights = weights_ref[part, :]
            pick = (across - off_ref[b] == down_j).astype(F32).astype(BF16)
            band_ref[part, :] = dot(weights, pick).astype(BF16)
            pick = (down - off_ref[b] == across_j).astype(F32).astype(BF16)
            turned_ref[:, part] = dot_t(pick, weights).astype(BF16)

    def half():
        return lax.axis_index("group") if groups == 2 else 0

    def open_up(
        off_hbm, weights_hbm, d_hbm, w_hbm, in_hbm, band_ref, turned_ref, d_vm, w_vm, x_ref, off, weights, sems
    ):
        at = lax.axis_index("tensor")
        loads = []

        def load(source, target):
            copy = pltpu.make_async_copy(source, target, sems.at[len(loads)])
            copy.start()
            loads.append(copy)

        load(off_hbm, off)
        load(weights_hbm, weights)
        for k, mask in enumerate((1, 3)):
            part = pl.ds(pl.multiple_of((at ^ mask) * width, width), width)
            load(w_hbm.at[part, :], w_vm.at[k])
            step = bytes_here // 4
            for q in (2 * k, 2 * k + 1):
                part = pl.ds(q * step, step)
                load(d_hbm.at[part, :], d_vm.at[part, :])
        quarter = at ^ 2 ^ half()
        load(in_hbm.at[pl.ds(pl.multiple_of(quarter * share, share), share), :], x_ref)
        for copy in loads[:2]:
            copy.wait()
        spread(off, weights, band_ref, turned_ref)
        for copy in loads[2:]:
            copy.wait()

    def grad_for_other(d_ref, w_ref, out_ref):
        for k in range(2):
            out_ref[:, k * width : (k + 1) * width] = dot_t(d_ref[...], w_ref[k]).astype(BF16)

    def fixed(value):
        return pltpu.with_memory_space_constraint(value, pltpu.HBM)

    band, turned, d_near, w_near, w_for_x = pl.pallas_call(
        open_up,
        out_shape=[
            shape((bytes_here, total_cols)),
            shape((total_cols, bytes_here)),
            shape((bytes_here, hidden)),
            shape((2, width, hidden)),
            shape((share, width)),
        ],
        in_specs=[pl.BlockSpec(memory_space=pltpu.HBM)] * 5,
        out_specs=[pl.BlockSpec(memory_space=pltpu.VMEM)] * 5,
        scratch_shapes=[
            pltpu.SMEM((blocks,), jnp.int32),
            pltpu.VMEM((bytes_here, breadth), BF16),
            pltpu.SemaphoreType.DMA((9,)),
        ],
        name="open_up",
        compiler_params=pltpu.CompilerParams(vmem_limit_bytes=16 << 20),
        cost_estimate=pl.CostEstimate(
            flops=4 * bytes_here * width * hidden,
            bytes_accessed=2 * (2 * width + bytes_here) * hidden,
            transcendentals=0,
        ),
    )(fixed(offsets), fixed(band_weights), fixed(d_up), fixed(w_up), fixed(w_in))
    w_x = swap(w_for_x, 2)
    product = 4 * bytes_here * width * hidden
    grad_sent, opened = call(
        grad_for_other,
        [shape((bytes_here, 2 * width))],
        d_near,
        w_near,
        flops=product,
        token=True,
    )
    grad_got = swap(grad_sent, 1)

    def project(spans_ref, w_ref, out_ref, *cut_refs):
        out_ref[...] = dot(spans_ref[...], w_ref[...]).astype(BF16)
        for ref, pairing in zip(cut_refs, longs):
            ref[...] = out_ref[pl.ds(cut_at(*pairing), far), :]

    reduced, *cuts, reduced_done = call(
        project,
        [shape((span_rows, width))] + [shape((far, width)) for _ in longs],
        spans,
        w_in,
        flops=2 * span_rows * depth * width,
        after=(opened,),
        token=True,
    )
    cut_of = dict(zip(longs, cuts))
    pieces = [reduced] + [trade(cut_of.get(p, reduced), p, count) for p in pairs]

    (grad_kept,) = call(
        functools.partial(grad_part, (0, 2)),
        [shape((bytes_here, 2 * width), F32)],
        d_near,
        w_up,
        flops=product,
        after=(reduced_done,),
    )

    def part_of(turned_ref, k, grad):
        return dot(turned_ref[cols[k] : cols[k] + rows[k], :], grad)

    def first_share(kept_ref, got_ref, turned_ref, grad_ref, out_ref):
        grad_ref[...] = (kept_ref[...] + got_ref[...].astype(F32)).astype(BF16)
        out_ref[...] = part_of(turned_ref, 1, grad_ref[...]).astype(BF16)

    def next_share(k, grad_ref, turned_ref, out_ref):
        out_ref[...] = part_of(turned_ref, k, grad_ref[...]).astype(out_ref.dtype)

    products = [2 * bytes_here * 2 * width * r for r in rows]
    grad, share_sent, share_done = call(
        first_share,
        [shape((bytes_here, 2 * width)), shape((rows[1], 2 * width))],
        grad_kept,
        grad_got,
        turned,
        flops=products[1],
        token=True,
    )
    came = [trade(share_sent, pairs[0], count)]
    for k in range(2, len(rows)):
        share_sent, share_done = call(
            functools.partial(next_share, k),
            [shape((rows[k], 2 * width))],
            grad,
            turned,
            flops=products[k],
            after=(share_done, *pieces[1:]) if k == len(rows) - 1 else (share_done,),
            token=True,
        )
        came.append(trade(share_sent, pairs[k - 1], count))
    own, own_done = call(
        functools.partial(next_share, 0),
        [shape((span_rows, 2 * width), F32)],
        grad,
        turned,
        flops=products[0],
        after=(share_done,),
        token=True,
    )

    def upsample(band_ref, *refs):
        *piece_refs, out_ref = refs
        acc = 0.0
        for k, ref in enumerate(piece_refs):
            acc += dot(band_ref[:, cols[k] : cols[k] + rows[k]], ref[...])
        out_ref[...] = acc.astype(BF16)

    (upsampled,) = call(
        upsample,
        [shape((bytes_here, width))],
        band,
        *pieces,
        flops=2 * bytes_here * width * sum(rows),
        after=(own_done, w_x),
    )
    up_x = swap(upsampled, 2)

    if groups == 2:
        w_y = lax.ppermute(w_x, "group", [(0, 1), (1, 0)])
    else:
        cube = w_in.reshape(4, share, width)
        w_y = swap(lax.dynamic_index_in_dim(cube, lax.axis_index("tensor") ^ 3, 0, keepdims=False), 2)

    def collect(own_ref, *refs):
        *came_refs, sum_ref, sent_ref = refs
        sum_ref[...] = own_ref[...]
        for ref, (distance, parity) in zip(came_refs, pairs):
            if distance == 1:
                sum_ref[...] += ref[...].astype(F32)
            else:
                sum_ref[pl.ds(cut_at(distance, parity), far), :] += ref[...].astype(F32)
        sent_ref[:, width:] = sum_ref[:, :width].astype(BF16)
        sent_ref[:, :width] = sum_ref[:, width:].astype(BF16)

    summed, sent = call(
        collect,
        [shape((span_rows, 2 * width), F32), shape((span_rows, 2 * width))],
        own,
        *came,
        flops=10**10,
    )

    over_x = swap(sent, 2)

    def up_near(own_ref, came_ref, w_ref, acc_ref):
        acc = dot(own_ref[...], block_of(w_ref, 0, width))
        acc_ref[...] = acc + dot(came_ref[...], block_of(w_ref, 2, width))

    (up_acc,) = call(
        up_near,
        [shape((bytes_here, hidden), F32)],
        upsampled,
        up_x,
        w_up,
        flops=product,
    )

    def pack(own_ref, came_ref, out_ref):
        out_ref[:, :width] = own_ref[...]
        out_ref[:, width:] = came_ref[...]

    (up_pair,) = call(pack, [shape((bytes_here, 2 * width))], upsampled, up_x, flops=bytes_here, after=(over_x, w_y, up_acc))
    up_other = swap(up_pair, 1)

    def combine(sum_ref, came_ref, out_ref):
        out_ref[...] = (sum_ref[...] + came_ref[...].astype(F32)).astype(BF16)

    (d_reduced,) = call(
        combine,
        [shape((span_rows, 2 * width))],
        summed,
        over_x,
        flops=2 * span_rows * width,
        after=(up_acc, w_y),
    )
    def finish_part(mask, mine_ref, w_ref, x_ref, y_ref, out_ref):
        first = groups != 2 or lax.axis_index("group") == 0
        near, far = (x_ref, y_ref) if mask == 0 else (y_ref, x_ref)
        across = near[...] if groups != 2 else jnp.where(first, near[...], far[...])
        part = dot_t(mine_ref[:, :width], block_of(w_ref, mask, share))
        out_ref[...] = (part + dot_t(mine_ref[:, width:], across)).astype(out_ref.dtype)

    def finish(mask, kind, after=()):
        return call(
            functools.partial(finish_part, mask),
            [shape((span_rows, share), kind)],
            d_reduced,
            w_in,
            w_x,
            w_y,
            flops=4 * span_rows * width * share,
            after=after,
        )[0]

    part_sent = finish(1, BF16)
    part_got = swap(part_sent, 1)
    part_kept = finish(0, F32, after=(part_sent,))

    def close(acc_ref, other_ref, w_ref, kept_ref, got_ref, up_hbm, spans_hbm, up_vm, spans_vm, sems):
        copies = []

        def store(source, target):
            copies.append(pltpu.make_async_copy(source, target, sems.at[len(copies)]))
            copies[-1].start()

        spans_vm[...] = (kept_ref[...] + got_ref[...].astype(F32)).astype(BF16)
        store(spans_vm, spans_hbm)
        step = bytes_here // 4
        for q in range(4):
            part = slice(q * step, (q + 1) * step)
            acc = acc_ref[part, :] + dot(other_ref[part, :width], block_of(w_ref, 1, width))
            acc += dot(other_ref[part, width:], block_of(w_ref, 3, width))
            up_vm[part, :] = acc.astype(BF16)
            part = pl.ds(q * step, step)
            store(up_vm.at[part, :], up_hbm.at[part, :])
        for copy in copies:
            copy.wait()

    up_proj, d_spans = pl.pallas_call(
        close,
        out_shape=[shape((bytes_here, hidden)), shape((span_rows, share))],
        in_specs=[pl.BlockSpec(memory_space=pltpu.VMEM)] * 5,
        out_specs=[pl.BlockSpec(memory_space=pltpu.HBM)] * 2,
        scratch_shapes=[
            pltpu.VMEM((bytes_here, hidden), BF16),
            pltpu.VMEM((span_rows, share), BF16),
            pltpu.SemaphoreType.DMA((5,)),
        ],
        name="close",
        compiler_params=pltpu.CompilerParams(vmem_limit_bytes=16 << 20),
        cost_estimate=pl.CostEstimate(
            flops=product, bytes_accessed=2 * bytes_here * hidden, transcendentals=0
        ),
    )(up_acc, up_other, w_up, part_kept, part_got)
    return (up_proj, d_spans)


def solution(mesh):
    placed = (
        P(("group", "seq"), None),
        P(None, "tensor"),
        P(("group", "seq"), None),
        P(("group", "seq")),
        P(None, "tensor"),
        P(("group", "seq"), "tensor"),
    )
    return jax.shard_map(
        body,
        mesh=mesh,
        in_specs=placed,
        out_specs=(P(("group", "seq"), "tensor"), P(("group", "seq"), "tensor")),
        check_vma=False,
    )
```

```python
import functools

import jax
import jax.numpy as jnp
from jax import lax
from jax.experimental import pallas as pl
from jax.experimental.pallas import tpu as pltpu
from jax.sharding import PartitionSpec as P

F32, BF16 = jnp.float32, jnp.bfloat16
PAD = 16
NOWHERE = -(1 << 20)


def reach(count, blocks, breadth, span_rows):
    usable = count * span_rows - breadth
    last = count * blocks - 1
    most = 0
    for index in range(count):
        low = max(index * blocks * usable // last - span_rows, 0)
        high = min(((index + 1) * blocks - 1) * usable // last + span_rows, usable) + breadth
        most = max(most, (index - 1) * span_rows - low, high - (index + 2) * span_rows)
    most = max(16, -(-most // 16) * 16)
    assert most <= span_rows
    return most


def pairings(count):
    every = [(1, 1), (2, 0), (2, 1), (1, 0)]
    return [p for p in every if any(partner(i, *p, count) != i for i in range(count))]


def partner(index, distance, parity, count):
    up = (index // distance) % 2 == parity
    other = index + distance if up else index - distance
    return other if 0 <= other < count else index


def partner_here(distance, parity, count):
    index = lax.axis_index("seq")
    up = lax.rem(lax.div(index, distance), 2) == parity
    other = jnp.where(up, index + distance, index - distance)
    return other, up, (other >= 0) & (other < count)


def trade(value, pairing, count):
    pairs = []
    for i in range(count):
        other = partner(i, *pairing, count)
        for t in range(4):
            pairs.append((4 * i + t, 4 * other + (t ^ 1 if other == i else t)))
    return lax.ppermute(value, ("seq", "tensor"), pairs)


def swap(value, mask):
    return lax.ppermute(value, "tensor", [(i, i ^ mask) for i in range(4)])


def call(kernel, outs, *args, flops, after=(), token=False):
    moved = sum(a.size * a.dtype.itemsize for a in args)
    moved += sum(o.size * o.dtype.itemsize for o in outs)
    spaces = [pltpu.VMEM] * len(args) + [pl.ANY] * len(after)
    inputs = len(args)
    outs = list(outs) + [shape((8, 128), F32)] * token

    def run(*refs):
        results = refs[inputs + len(after) :]
        if token:
            *results, token_ref = results
            token_ref[...] = jnp.zeros_like(token_ref)
        kernel(*refs[:inputs], *results)

    return pl.pallas_call(
        run,
        out_shape=outs,
        name=getattr(kernel, "func", kernel).__name__,
        in_specs=[pl.BlockSpec(memory_space=space) for space in spaces],
        out_specs=[pl.BlockSpec(memory_space=pltpu.VMEM)] * len(outs),
        compiler_params=pltpu.CompilerParams(vmem_limit_bytes=16 << 20),
        cost_estimate=pl.CostEstimate(flops=flops, bytes_accessed=moved, transcendentals=0),
    )(*args, *after)


def shape(dims, kind=BF16):
    return jax.ShapeDtypeStruct(dims, kind)


def dot(a, b):
    return jnp.dot(a, b, preferred_element_type=F32)


def dot_t(a, b):
    return lax.dot_general(a, b, (((1,), (1,)), ((), ())), preferred_element_type=F32)


def body(spans, w_in, band_weights, offsets, w_up, d_up):
    count = lax.axis_size("seq")
    groups = lax.axis_size("group")
    blocks, breadth = offsets.shape[0], band_weights.shape[1]
    bytes_here, hidden = d_up.shape
    block = bytes_here // blocks
    span_rows, depth = spans.shape
    width = w_in.shape[1]
    share = depth // 4
    far = reach(count, blocks, breadth, span_rows)
    pairs = pairings(count)
    rows = [span_rows] + [span_rows if d == 1 else far for d, _ in pairs]
    cols = [breadth * k for k in range(len(rows))]
    longs = [p for p in pairs if p[0] == 2]

    def cut_at(distance, parity):
        _, up, _ = partner_here(distance, parity, count)
        return pl.multiple_of(jnp.where(up, span_rows - far, 0), 16)

    def block_of(ref, mask, size):
        at = (lax.axis_index("tensor") ^ mask) * size
        return ref[pl.ds(pl.multiple_of(at, size), size), :]

    total_cols = breadth * len(rows)

    def grad_part(masks, d_ref, w_ref, out_ref):
        for k, mask in enumerate(masks):
            part = dot_t(d_ref[...], block_of(w_ref, mask, width))
            out_ref[:, k * width : (k + 1) * width] = part.astype(out_ref.dtype)

    def spread(off_ref, weights_ref, band_ref, turned_ref):
        starts = [lax.axis_index("seq") * span_rows]
        for distance, parity in pairs:
            other, up, there = partner_here(distance, parity, count)
            skip = 0 if distance == 1 else jnp.where(up, 0, span_rows - far)
            starts.append(jnp.where(there, other * span_rows + skip, NOWHERE))

        def row_ids(along):
            dims = (breadth, total_cols) if along else (total_cols, breadth)
            at = lax.broadcasted_iota(jnp.int32, dims, along)
            ids = NOWHERE
            for start, size, col in zip(starts, rows, cols):
                ids = jnp.where((at >= col) & (at < col + size), at + (start - col), ids)
            return ids, lax.broadcasted_iota(jnp.int32, dims, 1 - along)

        across, down_j = row_ids(1)
        down, across_j = row_ids(0)
        for b in range(blocks):
            part = slice(b * block, (b + 1) * block)
            weights = weights_ref[part, :]
            pick = (across - off_ref[b] == down_j).astype(F32).astype(BF16)
            band_ref[part, :] = dot(weights, pick).astype(BF16)
            pick = (down - off_ref[b] == across_j).astype(F32).astype(BF16)
            turned_ref[:, part] = dot_t(pick, weights).astype(BF16)

    def half():
        return lax.axis_index("group") if groups == 2 else 0

    def open_up(
        off_hbm, weights_hbm, d_hbm, w_hbm, in_hbm, band_ref, turned_ref, d_vm, w_vm, x_ref, off, weights, sems
    ):
        at = lax.axis_index("tensor")
        loads = []

        def load(source, target):
            copy = pltpu.make_async_copy(source, target, sems.at[len(loads)])
            copy.start()
            loads.append(copy)

        load(off_hbm, off)
        load(weights_hbm, weights)
        for k, mask in enumerate((1, 3)):
            part = pl.ds(pl.multiple_of((at ^ mask) * width, width), width)
            load(w_hbm.at[part, :], w_vm.at[k])
            step = bytes_here // 4
            for q in (2 * k, 2 * k + 1):
                part = pl.ds(q * step, step)
                load(d_hbm.at[part, :], d_vm.at[part, :])
        quarter = at ^ 2 ^ half()
        load(in_hbm.at[pl.ds(pl.multiple_of(quarter * share, share), share), :], x_ref)
        for copy in loads[:2]:
            copy.wait()
        spread(off, weights, band_ref, turned_ref)
        for copy in loads[2:]:
            copy.wait()

    def grad_for_other(d_ref, w_ref, out_ref):
        for k in range(2):
            out_ref[:, k * width : (k + 1) * width] = dot_t(d_ref[...], w_ref[k]).astype(BF16)

    def fixed(value):
        return pltpu.with_memory_space_constraint(value, pltpu.HBM)

    band, turned, d_near, w_near, w_for_x = pl.pallas_call(
        open_up,
        out_shape=[
            shape((bytes_here, total_cols)),
            shape((total_cols, bytes_here)),
            shape((bytes_here, hidden)),
            shape((2, width, hidden)),
            shape((share, width)),
        ],
        in_specs=[pl.BlockSpec(memory_space=pltpu.HBM)] * 5,
        out_specs=[pl.BlockSpec(memory_space=pltpu.VMEM)] * 5,
        scratch_shapes=[
            pltpu.SMEM((blocks,), jnp.int32),
            pltpu.VMEM((bytes_here, breadth), BF16),
            pltpu.SemaphoreType.DMA((9,)),
        ],
        name="open_up",
        compiler_params=pltpu.CompilerParams(vmem_limit_bytes=16 << 20),
        cost_estimate=pl.CostEstimate(
            flops=4 * bytes_here * width * hidden,
            bytes_accessed=2 * (2 * width + bytes_here) * hidden,
            transcendentals=0,
        ),
    )(fixed(offsets), fixed(band_weights), fixed(d_up), fixed(w_up), fixed(w_in))
    w_x = swap(w_for_x, 2)
    product = 4 * bytes_here * width * hidden
    grad_sent, opened = call(
        grad_for_other,
        [shape((bytes_here, 2 * width))],
        d_near,
        w_near,
        flops=product,
        token=True,
    )
    grad_got = swap(grad_sent, 1)

    def project(spans_ref, w_ref, out_ref, *cut_refs):
        out_ref[...] = dot(spans_ref[...], w_ref[...]).astype(BF16)
        for ref, pairing in zip(cut_refs, longs):
            ref[...] = out_ref[pl.ds(cut_at(*pairing), far), :]

    reduced, *cuts, reduced_done = call(
        project,
        [shape((span_rows, width))] + [shape((far, width)) for _ in longs],
        spans,
        w_in,
        flops=2 * span_rows * depth * width,
        after=(opened,),
        token=True,
    )
    cut_of = dict(zip(longs, cuts))
    pieces = [reduced] + [trade(cut_of.get(p, reduced), p, count) for p in pairs]

    (grad_kept,) = call(
        functools.partial(grad_part, (0, 2)),
        [shape((bytes_here, 2 * width), F32)],
        d_near,
        w_up,
        flops=product,
        after=(reduced_done,),
    )

    def part_of(turned_ref, k, grad):
        return dot(turned_ref[cols[k] : cols[k] + rows[k], :], grad)

    def first_share(kept_ref, got_ref, turned_ref, grad_ref, out_ref):
        grad_ref[...] = (kept_ref[...] + got_ref[...].astype(F32)).astype(BF16)
        out_ref[: rows[1], :] = part_of(turned_ref, 1, grad_ref[...]).astype(BF16)
        out_ref[rows[1] :, :] = jnp.zeros((PAD, 2 * width), BF16)

    def next_share(k, grad_ref, turned_ref, out_ref):
        out_ref[...] = part_of(turned_ref, k, grad_ref[...]).astype(out_ref.dtype)

    products = [2 * bytes_here * 2 * width * r for r in rows]
    grad, share_sent, share_done = call(
        first_share,
        [shape((bytes_here, 2 * width)), shape((rows[1] + PAD, 2 * width))],
        grad_kept,
        grad_got,
        turned,
        flops=products[1],
        token=True,
    )
    came = [trade(share_sent, pairs[0], count)]
    for k in range(2, len(rows)):
        share_sent, share_done = call(
            functools.partial(next_share, k),
            [shape((rows[k], 2 * width))],
            grad,
            turned,
            flops=products[k],
            after=(share_done, *pieces[1:]) if k == len(rows) - 1 else (share_done,),
            token=True,
        )
        came.append(trade(share_sent, pairs[k - 1], count))
    own, own_done = call(
        functools.partial(next_share, 0),
        [shape((span_rows, 2 * width), F32)],
        grad,
        turned,
        flops=products[0],
        after=(share_done,),
        token=True,
    )

    def upsample(band_ref, *refs):
        *piece_refs, out_ref = refs
        acc = 0.0
        for k, ref in enumerate(piece_refs):
            acc += dot(band_ref[:, cols[k] : cols[k] + rows[k]], ref[...])
        out_ref[...] = acc.astype(BF16)

    (upsampled,) = call(
        upsample,
        [shape((bytes_here, width))],
        band,
        *pieces,
        flops=2 * bytes_here * width * sum(rows),
        after=(own_done, w_x),
    )
    up_x = swap(upsampled, 2)

    if groups == 2:
        w_y = lax.ppermute(w_x, "group", [(0, 1), (1, 0)])
    else:
        cube = w_in.reshape(4, share, width)
        w_y = swap(lax.dynamic_index_in_dim(cube, lax.axis_index("tensor") ^ 3, 0, keepdims=False), 2)

    def collect(own_ref, *refs):
        *came_refs, sum_ref, sent_ref = refs
        sum_ref[...] = own_ref[...]
        for ref, (distance, parity) in zip(came_refs, pairs):
            if distance == 1:
                sum_ref[...] += ref[:span_rows, :].astype(F32)
            else:
                sum_ref[pl.ds(cut_at(distance, parity), far), :] += ref[...].astype(F32)
        sent_ref[:, width:] = sum_ref[:, :width].astype(BF16)
        sent_ref[:, :width] = sum_ref[:, width:].astype(BF16)

    summed, sent = call(
        collect,
        [shape((span_rows, 2 * width), F32), shape((span_rows, 2 * width))],
        own,
        *came,
        flops=10**10,
    )

    over_x = swap(sent, 2)

    def up_near(own_ref, came_ref, w_ref, acc_ref):
        acc = dot(own_ref[...], block_of(w_ref, 0, width))
        acc_ref[...] = acc + dot(came_ref[...], block_of(w_ref, 2, width))

    (up_acc,) = call(
        up_near,
        [shape((bytes_here, hidden), F32)],
        upsampled,
        up_x,
        w_up,
        flops=product,
    )

    def pack(own_ref, came_ref, out_ref):
        out_ref[:, :width] = own_ref[...]
        out_ref[:, width:] = came_ref[...]

    (up_pair,) = call(pack, [shape((bytes_here, 2 * width))], upsampled, up_x, flops=bytes_here, after=(over_x, w_y, up_acc))
    up_other = swap(up_pair, 1)

    def combine(sum_ref, came_ref, out_ref):
        out_ref[...] = (sum_ref[...] + came_ref[...].astype(F32)).astype(BF16)

    (d_reduced,) = call(
        combine,
        [shape((span_rows, 2 * width))],
        summed,
        over_x,
        flops=2 * span_rows * width,
        after=(up_acc, w_y),
    )
    def finish_part(mask, mine_ref, w_ref, x_ref, y_ref, out_ref):
        first = groups != 2 or lax.axis_index("group") == 0
        near, far = (x_ref, y_ref) if mask == 0 else (y_ref, x_ref)
        across = near[...] if groups != 2 else jnp.where(first, near[...], far[...])
        part = dot_t(mine_ref[:, :width], block_of(w_ref, mask, share))
        out_ref[...] = (part + dot_t(mine_ref[:, width:], across)).astype(out_ref.dtype)

    def finish(mask, kind, after=()):
        return call(
            functools.partial(finish_part, mask),
            [shape((span_rows, share), kind)],
            d_reduced,
            w_in,
            w_x,
            w_y,
            flops=4 * span_rows * width * share,
            after=after,
        )[0]

    part_sent = finish(1, BF16)
    part_got = swap(part_sent, 1)
    part_kept = finish(0, F32, after=(part_sent,))

    def close(acc_ref, other_ref, w_ref, kept_ref, got_ref, up_hbm, spans_hbm, up_vm, spans_vm, sems):
        copies = []

        def store(source, target):
            copies.append(pltpu.make_async_copy(source, target, sems.at[len(copies)]))
            copies[-1].start()

        spans_vm[...] = (kept_ref[...] + got_ref[...].astype(F32)).astype(BF16)
        store(spans_vm, spans_hbm)
        step = bytes_here // 4
        for q in range(4):
            part = slice(q * step, (q + 1) * step)
            acc = acc_ref[part, :] + dot(other_ref[part, :width], block_of(w_ref, 1, width))
            acc += dot(other_ref[part, width:], block_of(w_ref, 3, width))
            up_vm[part, :] = acc.astype(BF16)
            part = pl.ds(q * step, step)
            store(up_vm.at[part, :], up_hbm.at[part, :])
        for copy in copies:
            copy.wait()

    up_proj, d_spans = pl.pallas_call(
        close,
        out_shape=[shape((bytes_here, hidden)), shape((span_rows, share))],
        in_specs=[pl.BlockSpec(memory_space=pltpu.VMEM)] * 5,
        out_specs=[pl.BlockSpec(memory_space=pltpu.HBM)] * 2,
        scratch_shapes=[
            pltpu.VMEM((bytes_here, hidden), BF16),
            pltpu.VMEM((span_rows, share), BF16),
            pltpu.SemaphoreType.DMA((5,)),
        ],
        name="close",
        compiler_params=pltpu.CompilerParams(vmem_limit_bytes=16 << 20),
        cost_estimate=pl.CostEstimate(
            flops=product, bytes_accessed=2 * bytes_here * hidden, transcendentals=0
        ),
    )(up_acc, up_other, w_up, part_kept, part_got)
    return (up_proj, d_spans)


def solution(mesh):
    placed = (
        P(("group", "seq"), None),
        P(None, "tensor"),
        P(("group", "seq"), None),
        P(("group", "seq")),
        P(None, "tensor"),
        P(("group", "seq"), "tensor"),
    )
    return jax.shard_map(
        body,
        mesh=mesh,
        in_specs=placed,
        out_specs=(P(("group", "seq"), "tensor"), P(("group", "seq"), "tensor")),
        check_vma=False,
    )
```

```python
import functools

import jax
import jax.numpy as jnp
from jax import lax
from jax.experimental import pallas as pl
from jax.experimental.pallas import tpu as pltpu
from jax.sharding import PartitionSpec as P

F32, BF16 = jnp.float32, jnp.bfloat16
PAD = 16
NOWHERE = -(1 << 20)


def reach(count, blocks, breadth, span_rows):
    usable = count * span_rows - breadth
    last = count * blocks - 1
    most = 0
    for index in range(count):
        low = max(index * blocks * usable // last - span_rows, 0)
        high = min(((index + 1) * blocks - 1) * usable // last + span_rows, usable) + breadth
        most = max(most, (index - 1) * span_rows - low, high - (index + 2) * span_rows)
    most = max(16, -(-most // 16) * 16)
    assert most <= span_rows
    return most


def pairings(count):
    every = [(1, 1), (2, 0), (2, 1), (1, 0)]
    return [p for p in every if any(partner(i, *p, count) != i for i in range(count))]


def partner(index, distance, parity, count):
    up = (index // distance) % 2 == parity
    other = index + distance if up else index - distance
    return other if 0 <= other < count else index


def partner_here(distance, parity, count):
    index = lax.axis_index("seq")
    up = lax.rem(lax.div(index, distance), 2) == parity
    other = jnp.where(up, index + distance, index - distance)
    return other, up, (other >= 0) & (other < count)


def trade(value, pairing, count):
    pairs = []
    for i in range(count):
        other = partner(i, *pairing, count)
        for t in range(4):
            pairs.append((4 * i + t, 4 * other + (t ^ 1 if other == i else t)))
    return lax.ppermute(value, ("seq", "tensor"), pairs)


def swap(value, mask):
    return lax.ppermute(value, "tensor", [(i, i ^ mask) for i in range(4)])


def call(kernel, outs, *args, flops, after=(), token=False):
    moved = sum(a.size * a.dtype.itemsize for a in args)
    moved += sum(o.size * o.dtype.itemsize for o in outs)
    spaces = [pltpu.VMEM] * len(args) + [pl.ANY] * len(after)
    inputs = len(args)
    outs = list(outs) + [shape((8, 128), F32)] * token

    def run(*refs):
        results = refs[inputs + len(after) :]
        if token:
            *results, token_ref = results
            token_ref[...] = jnp.zeros_like(token_ref)
        kernel(*refs[:inputs], *results)

    return pl.pallas_call(
        run,
        out_shape=outs,
        name=getattr(kernel, "func", kernel).__name__,
        in_specs=[pl.BlockSpec(memory_space=space) for space in spaces],
        out_specs=[pl.BlockSpec(memory_space=pltpu.VMEM)] * len(outs),
        compiler_params=pltpu.CompilerParams(vmem_limit_bytes=16 << 20),
        cost_estimate=pl.CostEstimate(flops=flops, bytes_accessed=moved, transcendentals=0),
    )(*args, *after)


def shape(dims, kind=BF16):
    return jax.ShapeDtypeStruct(dims, kind)


def dot(a, b):
    return jnp.dot(a, b, preferred_element_type=F32)


def dot_t(a, b):
    return lax.dot_general(a, b, (((1,), (1,)), ((), ())), preferred_element_type=F32)


def body(spans, w_in, band_weights, offsets, w_up, d_up):
    count = lax.axis_size("seq")
    groups = lax.axis_size("group")
    blocks, breadth = offsets.shape[0], band_weights.shape[1]
    bytes_here, hidden = d_up.shape
    block = bytes_here // blocks
    span_rows, depth = spans.shape
    width = w_in.shape[1]
    share = depth // 4
    far = reach(count, blocks, breadth, span_rows)
    pairs = pairings(count)
    rows = [span_rows] + [span_rows if d == 1 else far for d, _ in pairs]
    cols = [breadth * k for k in range(len(rows))]
    longs = [p for p in pairs if p[0] == 2]

    def cut_at(distance, parity):
        _, up, _ = partner_here(distance, parity, count)
        return pl.multiple_of(jnp.where(up, span_rows - far, 0), 16)

    def block_of(ref, mask, size):
        at = (lax.axis_index("tensor") ^ mask) * size
        return ref[pl.ds(pl.multiple_of(at, size), size), :]

    total_cols = breadth * len(rows)

    def grad_part(masks, d_ref, w_ref, out_ref):
        for k, mask in enumerate(masks):
            part = dot_t(d_ref[...], block_of(w_ref, mask, width))
            out_ref[:, k * width : (k + 1) * width] = part.astype(out_ref.dtype)

    def spread(off_ref, weights_ref, band_ref, turned_ref):
        starts = [lax.axis_index("seq") * span_rows]
        for distance, parity in pairs:
            other, up, there = partner_here(distance, parity, count)
            skip = 0 if distance == 1 else jnp.where(up, 0, span_rows - far)
            starts.append(jnp.where(there, other * span_rows + skip, NOWHERE))

        def row_ids(along):
            dims = (breadth, total_cols) if along else (total_cols, breadth)
            at = lax.broadcasted_iota(jnp.int32, dims, along)
            ids = NOWHERE
            for start, size, col in zip(starts, rows, cols):
                ids = jnp.where((at >= col) & (at < col + size), at + (start - col), ids)
            return ids, lax.broadcasted_iota(jnp.int32, dims, 1 - along)

        across, down_j = row_ids(1)
        down, across_j = row_ids(0)
        for b in range(blocks):
            part = slice(b * block, (b + 1) * block)
            weights = weights_ref[part, :]
            pick = (across - off_ref[b] == down_j).astype(F32).astype(BF16)
            band_ref[part, :] = dot(weights, pick).astype(BF16)
            pick = (down - off_ref[b] == across_j).astype(F32).astype(BF16)
            turned_ref[:, part] = dot_t(pick, weights).astype(BF16)

    def half():
        return lax.axis_index("group") if groups == 2 else 0

    def open_up(
        off_hbm, weights_hbm, d_hbm, w_hbm, in_hbm, band_ref, turned_ref, d_vm, w_vm, x_ref, off, weights, sems
    ):
        at = lax.axis_index("tensor")
        loads = []

        def load(source, target):
            copy = pltpu.make_async_copy(source, target, sems.at[len(loads)])
            copy.start()
            loads.append(copy)

        load(off_hbm, off)
        load(weights_hbm, weights)
        for k, mask in enumerate((1, 3)):
            part = pl.ds(pl.multiple_of((at ^ mask) * width, width), width)
            load(w_hbm.at[part, :], w_vm.at[k])
            step = bytes_here // 4
            for q in (2 * k, 2 * k + 1):
                part = pl.ds(q * step, step)
                load(d_hbm.at[part, :], d_vm.at[part, :])
        quarter = at ^ 2 ^ half()
        load(in_hbm.at[pl.ds(pl.multiple_of(quarter * share, share), share), :], x_ref)
        for copy in loads[:2]:
            copy.wait()
        spread(off, weights, band_ref, turned_ref)
        for copy in loads[2:]:
            copy.wait()

    def grad_for_other(d_ref, w_ref, out_ref):
        for k in range(2):
            out_ref[:, k * width : (k + 1) * width] = dot_t(d_ref[...], w_ref[k]).astype(BF16)

    def fixed(value):
        return pltpu.with_memory_space_constraint(value, pltpu.HBM)

    band, turned, d_near, w_near, w_for_x = pl.pallas_call(
        open_up,
        out_shape=[
            shape((bytes_here, total_cols)),
            shape((total_cols, bytes_here)),
            shape((bytes_here, hidden)),
            shape((2, width, hidden)),
            shape((share, width)),
        ],
        in_specs=[pl.BlockSpec(memory_space=pltpu.HBM)] * 5,
        out_specs=[pl.BlockSpec(memory_space=pltpu.VMEM)] * 5,
        scratch_shapes=[
            pltpu.SMEM((blocks,), jnp.int32),
            pltpu.VMEM((bytes_here, breadth), BF16),
            pltpu.SemaphoreType.DMA((9,)),
        ],
        name="open_up",
        compiler_params=pltpu.CompilerParams(vmem_limit_bytes=16 << 20),
        cost_estimate=pl.CostEstimate(
            flops=4 * bytes_here * width * hidden,
            bytes_accessed=2 * (2 * width + bytes_here) * hidden,
            transcendentals=0,
        ),
    )(fixed(offsets), fixed(band_weights), fixed(d_up), fixed(w_up), fixed(w_in))
    w_x = swap(w_for_x, 2)
    product = 4 * bytes_here * width * hidden
    grad_sent, opened = call(
        grad_for_other,
        [shape((bytes_here, 2 * width))],
        d_near,
        w_near,
        flops=product,
        token=True,
    )
    grad_got = swap(grad_sent, 1)

    def project(spans_ref, w_ref, out_ref, *cut_refs):
        out_ref[...] = dot(spans_ref[...], w_ref[...]).astype(BF16)
        for ref, pairing in zip(cut_refs, longs):
            ref[...] = out_ref[pl.ds(cut_at(*pairing), far), :]

    reduced, *cuts, reduced_done = call(
        project,
        [shape((span_rows, width))] + [shape((far, width)) for _ in longs],
        spans,
        w_in,
        flops=2 * span_rows * depth * width,
        after=(opened,),
        token=True,
    )
    cut_of = dict(zip(longs, cuts))
    pieces = [reduced] + [trade(cut_of.get(p, reduced), p, count) for p in pairs]

    (grad_kept,) = call(
        functools.partial(grad_part, (0, 2)),
        [shape((bytes_here, 2 * width), F32)],
        d_near,
        w_up,
        flops=product,
        after=(reduced_done,),
    )

    def part_of(turned_ref, k, grad):
        return dot(turned_ref[cols[k] : cols[k] + rows[k], :], grad)

    def first_share(kept_ref, got_ref, turned_ref, grad_ref, out_ref):
        grad_ref[...] = (kept_ref[...] + got_ref[...].astype(F32)).astype(BF16)
        out_ref[: rows[1], :] = part_of(turned_ref, 1, grad_ref[...]).astype(BF16)
        out_ref[rows[1] :, :] = jnp.zeros((PAD, 2 * width), BF16)

    def next_share(k, grad_ref, turned_ref, out_ref):
        out_ref[...] = part_of(turned_ref, k, grad_ref[...]).astype(out_ref.dtype)

    products = [2 * bytes_here * 2 * width * r for r in rows]
    grad, share_sent, share_done = call(
        first_share,
        [shape((bytes_here, 2 * width)), shape((rows[1] + PAD, 2 * width))],
        grad_kept,
        grad_got,
        turned,
        flops=products[1],
        token=True,
    )
    first_done = share_done
    came = [trade(share_sent, pairs[0], count)]

    def upsample(band_ref, *refs):
        *piece_refs, out_ref = refs
        acc = 0.0
        for k, ref in enumerate(piece_refs):
            acc += dot(band_ref[:, cols[k] : cols[k] + rows[k]], ref[...])
        out_ref[...] = acc.astype(BF16)

    (upsampled,) = call(
        upsample,
        [shape((bytes_here, width))],
        band,
        *pieces,
        flops=2 * bytes_here * width * sum(rows),
        after=(first_done,),
    )
    up_x = swap(upsampled, 2)

    for k in range(2, len(rows)):
        share_sent, share_done = call(
            functools.partial(next_share, k),
            [shape((rows[k], 2 * width))],
            grad,
            turned,
            flops=products[k],
            after=(share_done, upsampled) if k == len(rows) - 1 else (share_done,),
            token=True,
        )
        came.append(trade(share_sent, pairs[k - 1], count))
    own, own_done = call(
        functools.partial(next_share, 0),
        [shape((span_rows, 2 * width), F32)],
        grad,
        turned,
        flops=products[0],
        after=(share_done, w_x),
        token=True,
    )


    if groups == 2:
        w_y = lax.ppermute(w_x, "group", [(0, 1), (1, 0)])
    else:
        cube = w_in.reshape(4, share, width)
        w_y = swap(lax.dynamic_index_in_dim(cube, lax.axis_index("tensor") ^ 3, 0, keepdims=False), 2)

    def collect(own_ref, *refs):
        *came_refs, sum_ref, sent_ref = refs
        sum_ref[...] = own_ref[...]
        for ref, (distance, parity) in zip(came_refs, pairs):
            if distance == 1:
                sum_ref[...] += ref[:span_rows, :].astype(F32)
            else:
                sum_ref[pl.ds(cut_at(distance, parity), far), :] += ref[...].astype(F32)
        sent_ref[:, width:] = sum_ref[:, :width].astype(BF16)
        sent_ref[:, :width] = sum_ref[:, width:].astype(BF16)

    summed, sent = call(
        collect,
        [shape((span_rows, 2 * width), F32), shape((span_rows, 2 * width))],
        own,
        *came,
        flops=10**10,
    )

    over_x = swap(sent, 2)

    def up_near(own_ref, came_ref, w_ref, acc_ref):
        acc = dot(own_ref[...], block_of(w_ref, 0, width))
        acc_ref[...] = acc + dot(came_ref[...], block_of(w_ref, 2, width))

    (up_acc,) = call(
        up_near,
        [shape((bytes_here, hidden), F32)],
        upsampled,
        up_x,
        w_up,
        flops=product,
    )

    def pack(own_ref, came_ref, out_ref):
        out_ref[:, :width] = own_ref[...]
        out_ref[:, width:] = came_ref[...]

    (up_pair,) = call(pack, [shape((bytes_here, 2 * width))], upsampled, up_x, flops=bytes_here, after=(over_x, w_y, up_acc))
    up_other = swap(up_pair, 1)

    def combine(sum_ref, came_ref, out_ref):
        out_ref[...] = (sum_ref[...] + came_ref[...].astype(F32)).astype(BF16)

    (d_reduced,) = call(
        combine,
        [shape((span_rows, 2 * width))],
        summed,
        over_x,
        flops=2 * span_rows * width,
        after=(up_acc, w_y),
    )
    def finish_part(mask, mine_ref, w_ref, x_ref, y_ref, out_ref):
        first = groups != 2 or lax.axis_index("group") == 0
        near, far = (x_ref, y_ref) if mask == 0 else (y_ref, x_ref)
        across = near[...] if groups != 2 else jnp.where(first, near[...], far[...])
        part = dot_t(mine_ref[:, :width], block_of(w_ref, mask, share))
        out_ref[...] = (part + dot_t(mine_ref[:, width:], across)).astype(out_ref.dtype)

    def finish(mask, kind, after=()):
        return call(
            functools.partial(finish_part, mask),
            [shape((span_rows, share), kind)],
            d_reduced,
            w_in,
            w_x,
            w_y,
            flops=4 * span_rows * width * share,
            after=after,
        )[0]

    part_sent = finish(1, BF16)
    part_got = swap(part_sent, 1)
    part_kept = finish(0, F32, after=(part_sent,))

    def close(acc_ref, other_ref, w_ref, kept_ref, got_ref, up_hbm, spans_hbm, up_vm, spans_vm, sems):
        copies = []

        def store(source, target):
            copies.append(pltpu.make_async_copy(source, target, sems.at[len(copies)]))
            copies[-1].start()

        spans_vm[...] = (kept_ref[...] + got_ref[...].astype(F32)).astype(BF16)
        store(spans_vm, spans_hbm)
        step = bytes_here // 4
        for q in range(4):
            part = slice(q * step, (q + 1) * step)
            acc = acc_ref[part, :] + dot(other_ref[part, :width], block_of(w_ref, 1, width))
            acc += dot(other_ref[part, width:], block_of(w_ref, 3, width))
            up_vm[part, :] = acc.astype(BF16)
            part = pl.ds(q * step, step)
            store(up_vm.at[part, :], up_hbm.at[part, :])
        for copy in copies:
            copy.wait()

    up_proj, d_spans = pl.pallas_call(
        close,
        out_shape=[shape((bytes_here, hidden)), shape((span_rows, share))],
        in_specs=[pl.BlockSpec(memory_space=pltpu.VMEM)] * 5,
        out_specs=[pl.BlockSpec(memory_space=pltpu.HBM)] * 2,
        scratch_shapes=[
            pltpu.VMEM((bytes_here, hidden), BF16),
            pltpu.VMEM((span_rows, share), BF16),
            pltpu.SemaphoreType.DMA((5,)),
        ],
        name="close",
        compiler_params=pltpu.CompilerParams(vmem_limit_bytes=16 << 20),
        cost_estimate=pl.CostEstimate(
            flops=product, bytes_accessed=2 * bytes_here * hidden, transcendentals=0
        ),
    )(up_acc, up_other, w_up, part_kept, part_got)
    return (up_proj, d_spans)


def solution(mesh):
    placed = (
        P(("group", "seq"), None),
        P(None, "tensor"),
        P(("group", "seq"), None),
        P(("group", "seq")),
        P(None, "tensor"),
        P(("group", "seq"), "tensor"),
    )
    return jax.shard_map(
        body,
        mesh=mesh,
        in_specs=placed,
        out_specs=(P(("group", "seq"), "tensor"), P(("group", "seq"), "tensor")),
        check_vma=False,
    )
```

```python
import functools

import jax
import jax.numpy as jnp
from jax import lax
from jax.experimental import pallas as pl
from jax.experimental.pallas import tpu as pltpu
from jax.sharding import PartitionSpec as P

F32, BF16 = jnp.float32, jnp.bfloat16
PAD = 16
NOWHERE = -(1 << 20)


def reach(count, blocks, breadth, span_rows):
    usable = count * span_rows - breadth
    last = count * blocks - 1
    most = 0
    for index in range(count):
        low = max(index * blocks * usable // last - span_rows, 0)
        high = min(((index + 1) * blocks - 1) * usable // last + span_rows, usable) + breadth
        most = max(most, (index - 1) * span_rows - low, high - (index + 2) * span_rows)
    most = max(16, -(-most // 16) * 16)
    assert most <= span_rows
    return most


def pairings(count):
    every = [(1, 1), (2, 0), (2, 1), (1, 0)]
    return [p for p in every if any(partner(i, *p, count) != i for i in range(count))]


def partner(index, distance, parity, count):
    up = (index // distance) % 2 == parity
    other = index + distance if up else index - distance
    return other if 0 <= other < count else index


def partner_here(distance, parity, count):
    index = lax.axis_index("seq")
    up = lax.rem(lax.div(index, distance), 2) == parity
    other = jnp.where(up, index + distance, index - distance)
    return other, up, (other >= 0) & (other < count)


def trade(value, pairing, count):
    pairs = []
    for i in range(count):
        other = partner(i, *pairing, count)
        for t in range(4):
            pairs.append((4 * i + t, 4 * other + (t ^ 1 if other == i else t)))
    return lax.ppermute(value, ("seq", "tensor"), pairs)


def swap(value, mask):
    return lax.ppermute(value, "tensor", [(i, i ^ mask) for i in range(4)])


def call(kernel, outs, *args, flops, after=(), token=False):
    moved = sum(a.size * a.dtype.itemsize for a in args)
    moved += sum(o.size * o.dtype.itemsize for o in outs)
    spaces = [pltpu.VMEM] * len(args) + [pl.ANY] * len(after)
    inputs = len(args)
    outs = list(outs) + [shape((8, 128), F32)] * token

    def run(*refs):
        results = refs[inputs + len(after) :]
        if token:
            *results, token_ref = results
            token_ref[...] = jnp.zeros_like(token_ref)
        kernel(*refs[:inputs], *results)

    return pl.pallas_call(
        run,
        out_shape=outs,
        name=getattr(kernel, "func", kernel).__name__,
        in_specs=[pl.BlockSpec(memory_space=space) for space in spaces],
        out_specs=[pl.BlockSpec(memory_space=pltpu.VMEM)] * len(outs),
        compiler_params=pltpu.CompilerParams(vmem_limit_bytes=16 << 20),
        cost_estimate=pl.CostEstimate(flops=flops, bytes_accessed=moved, transcendentals=0),
    )(*args, *after)


def shape(dims, kind=BF16):
    return jax.ShapeDtypeStruct(dims, kind)


def dot(a, b):
    return jnp.dot(a, b, preferred_element_type=F32)


def dot_t(a, b):
    return lax.dot_general(a, b, (((1,), (1,)), ((), ())), preferred_element_type=F32)


def body(spans, w_in, band_weights, offsets, w_up, d_up):
    count = lax.axis_size("seq")
    assert lax.axis_size("group") == 2 and lax.axis_size("tensor") == 4
    blocks, breadth = offsets.shape[0], band_weights.shape[1]
    bytes_here, hidden = d_up.shape
    block = bytes_here // blocks
    span_rows, depth = spans.shape
    width = w_in.shape[1]
    share = depth // 4
    far = reach(count, blocks, breadth, span_rows)
    pairs = pairings(count)
    rows = [span_rows] + [span_rows if d == 1 else far for d, _ in pairs]
    cols = [breadth * k for k in range(len(rows))]
    longs = [p for p in pairs if p[0] == 2]

    def cut_at(distance, parity):
        _, up, _ = partner_here(distance, parity, count)
        return pl.multiple_of(jnp.where(up, span_rows - far, 0), 16)

    def block_of(ref, mask, size):
        at = (lax.axis_index("tensor") ^ mask) * size
        return ref[pl.ds(pl.multiple_of(at, size), size), :]

    total_cols = breadth * len(rows)

    def grad_part(masks, d_ref, w_ref, out_ref):
        for k, mask in enumerate(masks):
            part = dot_t(d_ref[...], block_of(w_ref, mask, width))
            out_ref[:, k * width : (k + 1) * width] = part.astype(out_ref.dtype)

    def spread(off_ref, weights_ref, band_ref, turned_ref):
        starts = [lax.axis_index("seq") * span_rows]
        for distance, parity in pairs:
            other, up, there = partner_here(distance, parity, count)
            skip = 0 if distance == 1 else jnp.where(up, 0, span_rows - far)
            starts.append(jnp.where(there, other * span_rows + skip, NOWHERE))

        def row_ids(along):
            dims = (breadth, total_cols) if along else (total_cols, breadth)
            at = lax.broadcasted_iota(jnp.int32, dims, along)
            ids = NOWHERE
            for start, size, col in zip(starts, rows, cols):
                ids = jnp.where((at >= col) & (at < col + size), at + (start - col), ids)
            return ids, lax.broadcasted_iota(jnp.int32, dims, 1 - along)

        across, down_j = row_ids(1)
        down, across_j = row_ids(0)
        for b in range(blocks):
            part = slice(b * block, (b + 1) * block)
            weights = weights_ref[part, :]
            pick = (across - off_ref[b] == down_j).astype(F32).astype(BF16)
            band_ref[part, :] = dot(weights, pick).astype(BF16)
            pick = (down - off_ref[b] == across_j).astype(F32).astype(BF16)
            turned_ref[:, part] = dot_t(pick, weights).astype(BF16)

    unit = share // 6
    x_rows, y_rows = 7 * unit, 5 * unit

    def open_up(
        off_hbm, weights_hbm, d_hbm, w_hbm, in_hbm, band_ref, turned_ref, d_vm, w_vm, x_ref, off, weights, sems
    ):
        at = lax.axis_index("tensor")
        loads = []

        def load(source, target):
            copy = pltpu.make_async_copy(source, target, sems.at[len(loads)])
            copy.start()
            loads.append(copy)

        load(off_hbm, off)
        load(weights_hbm, weights)
        for k, mask in enumerate((1, 3)):
            part = pl.ds(pl.multiple_of((at ^ mask) * width, width), width)
            load(w_hbm.at[part, :], w_vm.at[k])
            step = bytes_here // 4
            for q in (2 * k, 2 * k + 1):
                part = pl.ds(q * step, step)
                load(d_hbm.at[part, :], d_vm.at[part, :])
        start = lax.div(at ^ 2, 2) * (2 * share) + lax.axis_index("group") * y_rows
        load(in_hbm.at[pl.ds(pl.multiple_of(start, unit), x_rows), :], x_ref)
        for copy in loads[:2]:
            copy.wait()
        spread(off, weights, band_ref, turned_ref)
        for copy in loads[2:]:
            copy.wait()

    def grad_for_other(d_ref, w_ref, out_ref):
        for k in range(2):
            out_ref[:, k * width : (k + 1) * width] = dot_t(d_ref[...], w_ref[k]).astype(BF16)

    def fixed(value):
        return pltpu.with_memory_space_constraint(value, pltpu.HBM)

    band, turned, d_near, w_near, w_for_x = pl.pallas_call(
        open_up,
        out_shape=[
            shape((bytes_here, total_cols)),
            shape((total_cols, bytes_here)),
            shape((bytes_here, hidden)),
            shape((2, width, hidden)),
            shape((x_rows, width)),
        ],
        in_specs=[pl.BlockSpec(memory_space=pltpu.HBM)] * 5,
        out_specs=[pl.BlockSpec(memory_space=pltpu.VMEM)] * 5,
        scratch_shapes=[
            pltpu.SMEM((blocks,), jnp.int32),
            pltpu.VMEM((bytes_here, breadth), BF16),
            pltpu.SemaphoreType.DMA((9,)),
        ],
        name="open_up",
        compiler_params=pltpu.CompilerParams(vmem_limit_bytes=16 << 20),
        cost_estimate=pl.CostEstimate(
            flops=4 * bytes_here * width * hidden,
            bytes_accessed=2 * (2 * width + bytes_here) * hidden,
            transcendentals=0,
        ),
    )(fixed(offsets), fixed(band_weights), fixed(d_up), fixed(w_up), fixed(w_in))
    w_x = swap(w_for_x, 2)
    product = 4 * bytes_here * width * hidden
    grad_sent, opened = call(
        grad_for_other,
        [shape((bytes_here, 2 * width))],
        d_near,
        w_near,
        flops=product,
        token=True,
    )
    grad_got = swap(grad_sent, 1)

    def project(spans_ref, w_ref, out_ref, wide_ref, *cut_refs):
        out_ref[...] = dot(spans_ref[...], w_ref[...]).astype(BF16)
        wide_ref[:span_rows, :] = out_ref[...]
        wide_ref[span_rows:, :] = jnp.zeros((PAD, width), BF16)
        for ref, pairing in zip(cut_refs, longs):
            ref[...] = out_ref[pl.ds(cut_at(*pairing), far), :]

    reduced, wide, *cuts, reduced_done = call(
        project,
        [shape((span_rows, width)), shape((span_rows + PAD, width))]
        + [shape((far, width)) for _ in longs],
        spans,
        w_in,
        flops=2 * span_rows * depth * width,
        after=(opened,),
        token=True,
    )
    cut_of = dict(zip(longs, cuts))
    cut_of[pairs[0]] = wide
    pieces = [reduced] + [trade(cut_of.get(p, reduced), p, count) for p in pairs]

    (grad_kept,) = call(
        functools.partial(grad_part, (0, 2)),
        [shape((bytes_here, 2 * width), F32)],
        d_near,
        w_up,
        flops=product,
        after=(reduced_done,),
    )

    def part_of(turned_ref, k, grad):
        return dot(turned_ref[cols[k] : cols[k] + rows[k], :], grad)

    def first_share(kept_ref, got_ref, turned_ref, grad_ref, out_ref):
        grad_ref[...] = (kept_ref[...] + got_ref[...].astype(F32)).astype(BF16)
        out_ref[: rows[1], :] = part_of(turned_ref, 1, grad_ref[...]).astype(BF16)
        out_ref[rows[1] :, :] = jnp.zeros((PAD, 2 * width), BF16)

    def next_share(k, grad_ref, turned_ref, out_ref):
        out_ref[...] = part_of(turned_ref, k, grad_ref[...]).astype(out_ref.dtype)

    products = [2 * bytes_here * 2 * width * r for r in rows]
    grad, share_sent, share_done = call(
        first_share,
        [shape((bytes_here, 2 * width)), shape((rows[1] + PAD, 2 * width))],
        grad_kept,
        grad_got,
        turned,
        flops=products[1],
        token=True,
    )
    first_done = share_done
    came = [trade(share_sent, pairs[0], count)]

    def upsample(band_ref, *refs):
        *piece_refs, out_ref = refs
        acc = 0.0
        for k, ref in enumerate(piece_refs):
            acc += dot(band_ref[:, cols[k] : cols[k] + rows[k]], ref[: rows[k], :])
        out_ref[...] = acc.astype(BF16)

    (upsampled,) = call(
        upsample,
        [shape((bytes_here, width))],
        band,
        *pieces,
        flops=2 * bytes_here * width * sum(rows),
        after=(first_done,),
    )
    up_x = swap(upsampled, 2)

    for k in range(2, len(rows)):
        share_sent, share_done = call(
            functools.partial(next_share, k),
            [shape((rows[k], 2 * width))],
            grad,
            turned,
            flops=products[k],
            after=(share_done, upsampled) if k == len(rows) - 1 else (share_done,),
            token=True,
        )
        came.append(trade(share_sent, pairs[k - 1], count))
    own, own_done = call(
        functools.partial(next_share, 0),
        [shape((span_rows, 2 * width), F32)],
        grad,
        turned,
        flops=products[0],
        after=(share_done, w_x),
        token=True,
    )


    def relay(w_ref, out_ref):
        start = lax.axis_index("group") * (x_rows - y_rows)
        out_ref[...] = w_ref[pl.ds(pl.multiple_of(start, unit), y_rows), :]

    (w_for_y,) = call(relay, [shape((y_rows, width))], w_x, flops=1, after=(upsampled,))
    w_y = lax.ppermute(w_for_y, "group", [(0, 1), (1, 0)])


    def collect(own_ref, *refs):
        *came_refs, sum_ref, sent_ref = refs
        sum_ref[...] = own_ref[...]
        for ref, (distance, parity) in zip(came_refs, pairs):
            if distance == 1:
                sum_ref[...] += ref[:span_rows, :].astype(F32)
            else:
                sum_ref[pl.ds(cut_at(distance, parity), far), :] += ref[...].astype(F32)
        sent_ref[:, width:] = sum_ref[:, :width].astype(BF16)
        sent_ref[:, :width] = sum_ref[:, width:].astype(BF16)

    summed, sent = call(
        collect,
        [shape((span_rows, 2 * width), F32), shape((span_rows, 2 * width))],
        own,
        *came,
        flops=10**10,
    )

    over_x = swap(sent, 2)

    def up_near(own_ref, came_ref, w_ref, acc_ref):
        acc = dot(own_ref[...], block_of(w_ref, 0, width))
        acc_ref[...] = acc + dot(came_ref[...], block_of(w_ref, 2, width))

    (up_acc,) = call(
        up_near,
        [shape((bytes_here, hidden), F32)],
        upsampled,
        up_x,
        w_up,
        flops=product,
    )

    def pack(own_ref, came_ref, out_ref):
        out_ref[:, :width] = own_ref[...]
        out_ref[:, width:] = came_ref[...]

    (up_pair,) = call(pack, [shape((bytes_here, 2 * width))], upsampled, up_x, flops=bytes_here, after=(over_x, w_y, up_acc))
    up_other = swap(up_pair, 1)

    def combine(sum_ref, came_ref, out_ref):
        out_ref[...] = (sum_ref[...] + came_ref[...].astype(F32)).astype(BF16)

    (d_reduced,) = call(
        combine,
        [shape((span_rows, 2 * width))],
        summed,
        over_x,
        flops=2 * span_rows * width,
        after=(up_acc, w_y),
    )
    def finish_part(mask, mine_ref, w_ref, x_ref, y_ref, out_ref):
        group = lax.axis_index("group")
        first = group == 0
        tiles = []
        for k in range(6):
            at = (lax.rem(lax.axis_index("tensor"), 2) ^ mask) * 6 + k
            x_at = jnp.clip(at - 5 * group, 0, 6) * unit
            y_at = jnp.clip(at - 7 * (1 - group), 0, 4) * unit
            x_tile = x_ref[pl.ds(pl.multiple_of(x_at, unit), unit), :]
            y_tile = y_ref[pl.ds(pl.multiple_of(y_at, unit), unit), :]
            by_x = (first & (at < 7)) | (~first & (at >= 5))
            tiles.append(jnp.where(by_x, x_tile, y_tile))
        across = jnp.concatenate(tiles, 0)
        part = dot_t(mine_ref[:, :width], block_of(w_ref, mask, share))
        out_ref[...] = (part + dot_t(mine_ref[:, width:], across)).astype(out_ref.dtype)

    def finish(mask, kind, after=()):
        return call(
            functools.partial(finish_part, mask),
            [shape((span_rows, share), kind)],
            d_reduced,
            w_in,
            w_x,
            w_y,
            flops=4 * span_rows * width * share,
            after=after,
        )[0]

    part_sent = finish(1, BF16)
    part_got = swap(part_sent, 1)
    part_kept = finish(0, F32, after=(part_sent,))

    def close(acc_ref, other_ref, w_ref, kept_ref, got_ref, up_hbm, spans_hbm, up_vm, spans_vm, sems):
        copies = []

        def store(source, target):
            copies.append(pltpu.make_async_copy(source, target, sems.at[len(copies)]))
            copies[-1].start()

        spans_vm[...] = (kept_ref[...] + got_ref[...].astype(F32)).astype(BF16)
        store(spans_vm, spans_hbm)
        step = bytes_here // 4
        for q in range(4):
            part = slice(q * step, (q + 1) * step)
            acc = acc_ref[part, :] + dot(other_ref[part, :width], block_of(w_ref, 1, width))
            acc += dot(other_ref[part, width:], block_of(w_ref, 3, width))
            up_vm[part, :] = acc.astype(BF16)
            part = pl.ds(q * step, step)
            store(up_vm.at[part, :], up_hbm.at[part, :])
        for copy in copies:
            copy.wait()

    up_proj, d_spans = pl.pallas_call(
        close,
        out_shape=[shape((bytes_here, hidden)), shape((span_rows, share))],
        in_specs=[pl.BlockSpec(memory_space=pltpu.VMEM)] * 5,
        out_specs=[pl.BlockSpec(memory_space=pltpu.HBM)] * 2,
        scratch_shapes=[
            pltpu.VMEM((bytes_here, hidden), BF16),
            pltpu.VMEM((span_rows, share), BF16),
            pltpu.SemaphoreType.DMA((5,)),
        ],
        name="close",
        compiler_params=pltpu.CompilerParams(vmem_limit_bytes=16 << 20),
        cost_estimate=pl.CostEstimate(
            flops=product, bytes_accessed=2 * bytes_here * hidden, transcendentals=0
        ),
    )(up_acc, up_other, w_up, part_kept, part_got)
    return (up_proj, d_spans)


def solution(mesh):
    placed = (
        P(("group", "seq"), None),
        P(None, "tensor"),
        P(("group", "seq"), None),
        P(("group", "seq")),
        P(None, "tensor"),
        P(("group", "seq"), "tensor"),
    )
    return jax.shard_map(
        body,
        mesh=mesh,
        in_specs=placed,
        out_specs=(P(("group", "seq"), "tensor"), P(("group", "seq"), "tensor")),
        check_vma=False,
    )
```

```python
import functools

import jax
import jax.numpy as jnp
from jax import lax
from jax.experimental import pallas as pl
from jax.experimental.pallas import tpu as pltpu
from jax.sharding import PartitionSpec as P

F32, BF16 = jnp.float32, jnp.bfloat16
PAD = 16
NOWHERE = -(1 << 20)


def reach(count, blocks, breadth, span_rows):
    usable = count * span_rows - breadth
    last = count * blocks - 1
    most = 0
    for index in range(count):
        low = max(index * blocks * usable // last - span_rows, 0)
        high = min(((index + 1) * blocks - 1) * usable // last + span_rows, usable) + breadth
        most = max(most, (index - 1) * span_rows - low, high - (index + 2) * span_rows)
    most = max(16, -(-most // 16) * 16)
    assert most <= span_rows
    return most


def pairings(count):
    every = [(1, 1), (2, 0), (2, 1), (1, 0)]
    return [p for p in every if any(partner(i, *p, count) != i for i in range(count))]


def partner(index, distance, parity, count):
    up = (index // distance) % 2 == parity
    other = index + distance if up else index - distance
    return other if 0 <= other < count else index


def partner_here(distance, parity, count):
    index = lax.axis_index("seq")
    up = lax.rem(lax.div(index, distance), 2) == parity
    other = jnp.where(up, index + distance, index - distance)
    return other, up, (other >= 0) & (other < count)


def trade(value, pairing, count):
    pairs = []
    for i in range(count):
        other = partner(i, *pairing, count)
        for t in range(4):
            pairs.append((4 * i + t, 4 * other + (t ^ 1 if other == i else t)))
    return lax.ppermute(value, ("seq", "tensor"), pairs)


def swap(value, mask):
    return lax.ppermute(value, "tensor", [(i, i ^ mask) for i in range(4)])


def call(kernel, outs, *args, flops, after=(), token=False):
    moved = sum(a.size * a.dtype.itemsize for a in args)
    moved += sum(o.size * o.dtype.itemsize for o in outs)
    spaces = [pltpu.VMEM] * len(args) + [pl.ANY] * len(after)
    inputs = len(args)
    outs = list(outs) + [shape((8, 128), F32)] * token

    def run(*refs):
        results = refs[inputs + len(after) :]
        if token:
            *results, token_ref = results
            token_ref[...] = jnp.zeros_like(token_ref)
        kernel(*refs[:inputs], *results)

    return pl.pallas_call(
        run,
        out_shape=outs,
        name=getattr(kernel, "func", kernel).__name__,
        in_specs=[pl.BlockSpec(memory_space=space) for space in spaces],
        out_specs=[pl.BlockSpec(memory_space=pltpu.VMEM)] * len(outs),
        compiler_params=pltpu.CompilerParams(vmem_limit_bytes=16 << 20),
        cost_estimate=pl.CostEstimate(flops=flops, bytes_accessed=moved, transcendentals=0),
    )(*args, *after)


def shape(dims, kind=BF16):
    return jax.ShapeDtypeStruct(dims, kind)


def dot(a, b):
    return jnp.dot(a, b, preferred_element_type=F32)


def dot_t(a, b):
    return lax.dot_general(a, b, (((1,), (1,)), ((), ())), preferred_element_type=F32)


def body(spans, w_in, band_weights, offsets, w_up, d_up):
    count = lax.axis_size("seq")
    assert lax.axis_size("group") == 2 and lax.axis_size("tensor") == 4
    blocks, breadth = offsets.shape[0], band_weights.shape[1]
    bytes_here, hidden = d_up.shape
    block = bytes_here // blocks
    span_rows, depth = spans.shape
    width = w_in.shape[1]
    share = depth // 4
    far = reach(count, blocks, breadth, span_rows)
    pairs = pairings(count)
    rows = [span_rows] + [span_rows if d == 1 else far for d, _ in pairs]
    cols = [breadth * k for k in range(len(rows))]
    longs = [p for p in pairs if p[0] == 2]

    def cut_at(distance, parity):
        _, up, _ = partner_here(distance, parity, count)
        return pl.multiple_of(jnp.where(up, span_rows - far, 0), 16)

    def block_of(ref, mask, size):
        at = (lax.axis_index("tensor") ^ mask) * size
        return ref[pl.ds(pl.multiple_of(at, size), size), :]

    total_cols = breadth * len(rows)

    def grad_part(masks, d_ref, w_ref, out_ref):
        for k, mask in enumerate(masks):
            part = dot_t(d_ref[...], block_of(w_ref, mask, width))
            out_ref[:, k * width : (k + 1) * width] = part.astype(out_ref.dtype)

    def spread(off_ref, weights_ref, band_ref, turned_ref):
        starts = [lax.axis_index("seq") * span_rows]
        for distance, parity in pairs:
            other, up, there = partner_here(distance, parity, count)
            skip = 0 if distance == 1 else jnp.where(up, 0, span_rows - far)
            starts.append(jnp.where(there, other * span_rows + skip, NOWHERE))

        def row_ids(along):
            dims = (breadth, total_cols) if along else (total_cols, breadth)
            at = lax.broadcasted_iota(jnp.int32, dims, along)
            ids = NOWHERE
            for start, size, col in zip(starts, rows, cols):
                ids = jnp.where((at >= col) & (at < col + size), at + (start - col), ids)
            return ids, lax.broadcasted_iota(jnp.int32, dims, 1 - along)

        across, down_j = row_ids(1)
        down, across_j = row_ids(0)
        for b in range(blocks):
            part = slice(b * block, (b + 1) * block)
            weights = weights_ref[part, :]
            pick = (across - off_ref[b] == down_j).astype(F32).astype(BF16)
            band_ref[part, :] = dot(weights, pick).astype(BF16)
            pick = (down - off_ref[b] == across_j).astype(F32).astype(BF16)
            turned_ref[:, part] = dot_t(pick, weights).astype(BF16)

    unit = share // 6
    x_rows, y_rows = 7 * unit, 5 * unit

    def open_up(
        off_hbm, weights_hbm, d_hbm, w_hbm, in_hbm, band_ref, turned_ref, d_vm, w_vm, x_ref, off, weights, sems
    ):
        at = lax.axis_index("tensor")
        loads = []

        def load(source, target):
            copy = pltpu.make_async_copy(source, target, sems.at[len(loads)])
            copy.start()
            loads.append(copy)

        load(off_hbm, off)
        load(weights_hbm, weights)
        for k, mask in enumerate((1, 3)):
            part = pl.ds(pl.multiple_of((at ^ mask) * width, width), width)
            load(w_hbm.at[part, :], w_vm.at[k])
            step = bytes_here // 4
            for q in (2 * k, 2 * k + 1):
                part = pl.ds(q * step, step)
                load(d_hbm.at[part, :], d_vm.at[part, :])
        start = lax.div(at ^ 2, 2) * (2 * share) + lax.axis_index("group") * y_rows
        load(in_hbm.at[pl.ds(pl.multiple_of(start, unit), x_rows), :], x_ref)
        for copy in loads[:2]:
            copy.wait()
        spread(off, weights, band_ref, turned_ref)
        for copy in loads[2:]:
            copy.wait()

    def grad_for_other(d_ref, w_ref, out_ref):
        for k in range(2):
            out_ref[:, k * width : (k + 1) * width] = dot_t(d_ref[...], w_ref[k]).astype(BF16)

    def fixed(value):
        return pltpu.with_memory_space_constraint(value, pltpu.HBM)

    band, turned, d_near, w_near, w_for_x = pl.pallas_call(
        open_up,
        out_shape=[
            shape((bytes_here, total_cols)),
            shape((total_cols, bytes_here)),
            shape((bytes_here, hidden)),
            shape((2, width, hidden)),
            shape((x_rows, width)),
        ],
        in_specs=[pl.BlockSpec(memory_space=pltpu.HBM)] * 5,
        out_specs=[pl.BlockSpec(memory_space=pltpu.VMEM)] * 5,
        scratch_shapes=[
            pltpu.SMEM((blocks,), jnp.int32),
            pltpu.VMEM((bytes_here, breadth), BF16),
            pltpu.SemaphoreType.DMA((9,)),
        ],
        name="open_up",
        compiler_params=pltpu.CompilerParams(vmem_limit_bytes=16 << 20),
        cost_estimate=pl.CostEstimate(
            flops=4 * bytes_here * width * hidden,
            bytes_accessed=2 * (2 * width + bytes_here) * hidden,
            transcendentals=0,
        ),
    )(fixed(offsets), fixed(band_weights), fixed(d_up), fixed(w_up), fixed(w_in))
    w_x = swap(w_for_x, 2)
    product = 4 * bytes_here * width * hidden
    grad_sent, opened = call(
        grad_for_other,
        [shape((bytes_here, 2 * width))],
        d_near,
        w_near,
        flops=product,
        token=True,
    )
    grad_got = swap(grad_sent, 1)

    def project(spans_ref, w_ref, out_ref, wide_ref, *cut_refs):
        out_ref[...] = dot(spans_ref[...], w_ref[...]).astype(BF16)
        wide_ref[:span_rows, :] = out_ref[...]
        wide_ref[span_rows:, :] = jnp.zeros((PAD, width), BF16)
        for ref, pairing in zip(cut_refs, longs):
            ref[...] = out_ref[pl.ds(cut_at(*pairing), far), :]

    reduced, wide, *cuts, reduced_done = call(
        project,
        [shape((span_rows, width)), shape((span_rows + PAD, width))]
        + [shape((far, width)) for _ in longs],
        spans,
        w_in,
        flops=2 * span_rows * depth * width,
        after=(opened,),
        token=True,
    )
    cut_of = dict(zip(longs, cuts))
    cut_of[pairs[0]] = wide
    pieces = [reduced] + [trade(cut_of.get(p, reduced), p, count) for p in pairs]

    (grad_kept,) = call(
        functools.partial(grad_part, (0, 2)),
        [shape((bytes_here, 2 * width), F32)],
        d_near,
        w_up,
        flops=product,
        after=(reduced_done,),
    )

    def part_of(turned_ref, k, grad):
        return dot(turned_ref[cols[k] : cols[k] + rows[k], :], grad)

    def first_share(kept_ref, got_ref, turned_ref, grad_ref, out_ref):
        grad_ref[...] = (kept_ref[...] + got_ref[...].astype(F32)).astype(BF16)
        out_ref[: rows[1], :] = part_of(turned_ref, 1, grad_ref[...]).astype(BF16)
        out_ref[rows[1] :, :] = jnp.zeros((PAD, 2 * width), BF16)

    def next_share(k, grad_ref, turned_ref, out_ref):
        out_ref[...] = part_of(turned_ref, k, grad_ref[...]).astype(out_ref.dtype)

    products = [2 * bytes_here * 2 * width * r for r in rows]
    grad, share_sent, share_done = call(
        first_share,
        [shape((bytes_here, 2 * width)), shape((rows[1] + PAD, 2 * width))],
        grad_kept,
        grad_got,
        turned,
        flops=products[1],
        token=True,
    )
    first_done = share_done
    came = [trade(share_sent, pairs[0], count)]

    def upsample(band_ref, *refs):
        *piece_refs, out_ref = refs
        acc = 0.0
        for k, ref in enumerate(piece_refs):
            acc += dot(band_ref[:, cols[k] : cols[k] + rows[k]], ref[: rows[k], :])
        out_ref[...] = acc.astype(BF16)

    (upsampled,) = call(
        upsample,
        [shape((bytes_here, width))],
        band,
        *pieces,
        flops=2 * bytes_here * width * sum(rows),
        after=(first_done,),
    )
    up_x = swap(upsampled, 2)

    for k in range(2, len(rows)):
        share_sent, share_done = call(
            functools.partial(next_share, k),
            [shape((rows[k], 2 * width))],
            grad,
            turned,
            flops=products[k],
            after=(share_done, upsampled) if k == len(rows) - 1 else (share_done,),
            token=True,
        )
        came.append(trade(share_sent, pairs[k - 1], count))
    own, own_done = call(
        functools.partial(next_share, 0),
        [shape((span_rows, 2 * width), F32)],
        grad,
        turned,
        flops=products[0],
        after=(share_done, w_x),
        token=True,
    )


    def relay(w_ref, out_ref):
        start = lax.axis_index("group") * (x_rows - y_rows)
        out_ref[...] = w_ref[pl.ds(pl.multiple_of(start, unit), y_rows), :]

    (w_for_y,) = call(relay, [shape((y_rows, width))], w_x, flops=1, after=(upsampled,))
    w_y = lax.ppermute(w_for_y, "group", [(0, 1), (1, 0)])


    def collect(own_ref, *refs):
        *came_refs, sum_ref, sent_ref = refs
        sum_ref[...] = own_ref[...]
        for ref, (distance, parity) in zip(came_refs, pairs):
            if distance == 1:
                sum_ref[...] += ref[:span_rows, :].astype(F32)
            else:
                sum_ref[pl.ds(cut_at(distance, parity), far), :] += ref[...].astype(F32)
        sent_ref[:, width:] = sum_ref[:, :width].astype(BF16)
        sent_ref[:, :width] = sum_ref[:, width:].astype(BF16)

    summed, sent = call(
        collect,
        [shape((span_rows, 2 * width), F32), shape((span_rows, 2 * width))],
        own,
        *came,
        flops=10**10,
    )

    over_x = swap(sent, 2)

    def up_near(own_ref, came_ref, w_ref, acc_ref):
        acc = dot(own_ref[...], block_of(w_ref, 0, width))
        acc_ref[...] = acc + dot(came_ref[...], block_of(w_ref, 2, width))

    (up_acc,) = call(
        up_near,
        [shape((bytes_here, hidden), F32)],
        upsampled,
        up_x,
        w_up,
        flops=product,
    )

    def pack(own_ref, came_ref, out_ref):
        out_ref[:, :width] = own_ref[...]
        out_ref[:, width:] = came_ref[...]

    (up_pair,) = call(pack, [shape((bytes_here, 2 * width))], upsampled, up_x, flops=bytes_here, after=(over_x, w_y, up_acc))
    up_other = swap(up_pair, 1)

    def combine(sum_ref, came_ref, out_ref):
        out_ref[...] = (sum_ref[...] + came_ref[...].astype(F32)).astype(BF16)

    (d_reduced,) = call(
        combine,
        [shape((span_rows, 2 * width))],
        summed,
        over_x,
        flops=2 * span_rows * width,
        after=(up_acc, w_y),
    )
    def finish_part(mask, mine_ref, w_ref, x_ref, y_ref, out_ref):
        group = lax.axis_index("group")
        first = group == 0
        tiles = []
        for k in range(6):
            at = (lax.rem(lax.axis_index("tensor"), 2) ^ mask) * 6 + k
            x_at = jnp.clip(at - 5 * group, 0, 6) * unit
            y_at = jnp.clip(at - 7 * (1 - group), 0, 4) * unit
            x_tile = x_ref[pl.ds(pl.multiple_of(x_at, unit), unit), :]
            y_tile = y_ref[pl.ds(pl.multiple_of(y_at, unit), unit), :]
            by_x = (first & (at < 7)) | (~first & (at >= 5))
            tiles.append(jnp.where(by_x, x_tile, y_tile))
        across = jnp.concatenate(tiles, 0)
        part = dot_t(mine_ref[:, :width], block_of(w_ref, mask, share))
        out_ref[...] = (part + dot_t(mine_ref[:, width:], across)).astype(out_ref.dtype)

    def finish(mask, kind, after=()):
        return call(
            functools.partial(finish_part, mask),
            [shape((span_rows, share), kind)],
            d_reduced,
            w_in,
            w_x,
            w_y,
            flops=4 * span_rows * width * share,
            after=after,
        )[0]

    part_sent = finish(1, BF16)
    part_got = swap(part_sent, 1)
    part_kept = finish(0, F32, after=(part_sent,))

    def close(acc_ref, other_ref, w_ref, kept_ref, got_ref, up_hbm, spans_hbm, up_vm, spans_vm, sems):
        copies = []

        def store(source, target):
            copies.append(pltpu.make_async_copy(source, target, sems.at[len(copies)]))
            copies[-1].start()

        spans_vm[...] = (kept_ref[...] + got_ref[...].astype(F32)).astype(BF16)
        store(spans_vm, spans_hbm)
        step = bytes_here // 2
        for q in range(2):
            part = slice(q * step, (q + 1) * step)
            acc = acc_ref[part, :] + dot(other_ref[part, :width], block_of(w_ref, 1, width))
            acc += dot(other_ref[part, width:], block_of(w_ref, 3, width))
            up_vm[part, :] = acc.astype(BF16)
            part = pl.ds(q * step, step)
            store(up_vm.at[part, :], up_hbm.at[part, :])
        for copy in copies:
            copy.wait()

    up_proj, d_spans = pl.pallas_call(
        close,
        out_shape=[shape((bytes_here, hidden)), shape((span_rows, share))],
        in_specs=[pl.BlockSpec(memory_space=pltpu.VMEM)] * 5,
        out_specs=[pl.BlockSpec(memory_space=pltpu.HBM)] * 2,
        scratch_shapes=[
            pltpu.VMEM((bytes_here, hidden), BF16),
            pltpu.VMEM((span_rows, share), BF16),
            pltpu.SemaphoreType.DMA((3,)),
        ],
        name="close",
        compiler_params=pltpu.CompilerParams(vmem_limit_bytes=16 << 20),
        cost_estimate=pl.CostEstimate(
            flops=product, bytes_accessed=2 * bytes_here * hidden, transcendentals=0
        ),
    )(up_acc, up_other, w_up, part_kept, part_got)
    return (up_proj, d_spans)


def solution(mesh):
    placed = (
        P(("group", "seq"), None),
        P(None, "tensor"),
        P(("group", "seq"), None),
        P(("group", "seq")),
        P(None, "tensor"),
        P(("group", "seq"), "tensor"),
    )
    return jax.shard_map(
        body,
        mesh=mesh,
        in_specs=placed,
        out_specs=(P(("group", "seq"), "tensor"), P(("group", "seq"), "tensor")),
        check_vma=False,
    )
```
